128 devices in a mesh: orb: 128 (over z, x, y, core).
Axes of the slice: x: 4, y: 4, z: 4, core: 2. Of those that a mesh axis runs over, the one named last changes fastest.
Arguments:
- orbitals: bfloat16 [512, 64, 4096], P('orb'), may hold values from -6 to 6
- pair_list: int32 [2048, 2], P('orb'), may hold values from 0 to 15, as said below
- pair_counts: int32 [128], P('orb'), may hold values from 1 to 16, as said below
Outputs:
- exchange_field: float32 [512, 64, 4096], P('orb')
The draws below stay inside these ranges and needn't reach their ends.
Inputs may be any that keep to these rules, and one draw needn't show every extreme that they name: `pair_list`: in each row (a, w) of a device's block, a is one of its own 4 orbitals and w is below (4) * 4; where w < 4 both orbitals are the device's own and w >= a. The rows of one device's block are distinct. `pair_counts`: some device's count is 16; rows past a device's count are not used.
All inputs are finite; a program needn't handle non-finite values.
Results may differ from the reference program's by a relative error of at most 0.0003.
Values may be sent and summed in bfloat16 or wider, within the bound.
A program may use at most 128 MiB of HBM per device.

```python
import math
import jax
import jax.numpy as jnp
import numpy as np
from jax import lax

B = 64
ORB_DEV = 4
PAIR_DEV = 16
REACH = 3
ORBITALS = 512
N_ORB = 128


def candidate_table():
    local_pairs = [(a, b) for a in range(ORB_DEV) for b in range(a, ORB_DEV)]
    ahead_pairs = [(a, ORB_DEV + k) for a in range(ORB_DEV) for k in range(REACH * ORB_DEV)]
    return np.array(local_pairs + ahead_pairs, dtype=np.int32)


def draw_pair_list(key, part):
    table = jnp.asarray(candidate_table())
    keys = jax.random.split(jax.random.fold_in(key, 11), N_ORB)
    chosen = jax.vmap(lambda k: jax.random.permutation(k, table.shape[0])[:PAIR_DEV])(keys)
    return table[chosen.reshape(-1)].astype(jnp.int32)


def draw_pair_counts(key, part):
    base = jax.random.randint(jax.random.fold_in(key, 23), (N_ORB,), 1, PAIR_DEV // 2 + 1)
    quarter = jax.random.randint(jax.random.fold_in(key, 31), (N_ORB,), 0, 4)
    chosen = jax.random.randint(jax.random.fold_in(key, 29), (), 0, N_ORB)
    filled = (quarter == 0) | (jnp.arange(N_ORB) == chosen)
    return jnp.where(filled, PAIR_DEV, base).astype(jnp.int32)


def levels(key, dims, pieces, least, largest):
    def one(axis_at, shards_of):
        draws = jax.random.uniform(jax.random.fold_in(jax.random.fold_in(key, 6), axis_at), (shards_of,), jnp.float32, least / len(pieces), largest / len(pieces))
        return jnp.repeat(jnp.exp(draws), dims[axis_at] // shards_of).reshape((-1,) + (1,) * (len(dims) - axis_at - 1))

    factor_of = one(*pieces[0])
    for cut in pieces[1:]:
        factor_of = factor_of * one(*cut)
    return factor_of


def centred(own_key, extent, width, bound, pieces=(), kind=jnp.bfloat16):
    values = jax.random.normal(own_key, extent, jnp.float32) * width
    if len(pieces) > 0:
        values = levels(own_key, extent, pieces, -0.22, 0.18) * values
    return jnp.clip(values, min=-bound, max=bound).astype(kind)


def setup_inputs(seed: int = 0) -> dict:
    key_list = jax.random.split(jax.random.key(seed), 4)
    return {
        "orbitals": centred(key_list[0], (ORBITALS, B, B * B), 1.0, 6.0, ((0, 128),)),
        "pair_list": draw_pair_list(jax.random.fold_in(key_list[3], 71), 0),
        "pair_counts": draw_pair_counts(jax.random.fold_in(key_list[3], 71), 0),
    }


screening = 0.5


def sine_table(points):
    modes = jnp.arange(points, dtype=jnp.float32) + 1.0
    return jnp.sin(math.pi * modes[:, None] * modes[None, :] / (points + 1))


def inverse_denominators(points):
    modes = jnp.arange(points, dtype=jnp.float32) + 1.0
    eigen = 4.0 * jnp.sin(math.pi * modes / (2.0 * (points + 1))) ** 2
    total = eigen[:, None, None] + eigen[None, :, None] + eigen[None, None, :] + screening
    return ((2.0 / (points + 1)) ** 3 / total).reshape(points, points * points)


def sine_cube(fields, sines):
    points = sines.shape[0]
    cube = fields.reshape(points, points, points)
    highest = lax.Precision.HIGHEST
    cube = jnp.einsum("kx,xyz->kyz", sines, cube, precision=highest)
    cube = jnp.einsum("ky,xyz->xkz", sines, cube, precision=highest)
    cube = jnp.einsum("kz,xyz->xyk", sines, cube, precision=highest)
    return cube.reshape(points, points * points)


def screened_potential(density, sines, inverse):
    return sine_cube(sine_cube(density, sines) * inverse, sines)


def reference(orbitals, pair_list, pair_counts):
    box_side = orbitals.shape[1]
    sines = sine_table(box_side)
    inverse = inverse_denominators(box_side)
    orbital_total = orbitals.shape[0]
    own_count = orbital_total // N_ORB
    fields = jnp.zeros(orbitals.shape, jnp.float32)

    def add_pair(slot_index, fields):
        device = slot_index // PAIR_DEV
        slot = slot_index % PAIR_DEV
        target = device * own_count + pair_list[slot_index, 0]
        partner = (device * own_count + pair_list[slot_index, 1]) % orbital_total

        def live_pair(fields):
            one_side = orbitals[target].astype(jnp.float32)
            other_side = orbitals[partner].astype(jnp.float32)
            potential = screened_potential(one_side * other_side, sines, inverse)
            fields = fields.at[target].add(potential * other_side)
            weight = (target != partner).astype(jnp.float32)
            return fields.at[partner].add(potential * one_side * weight)

        return lax.cond(slot < pair_counts[device], live_pair, lambda kept: kept, fields)

    fields = lax.fori_loop(0, pair_list.shape[0], add_pair, fields)
    return -fields
```

```python
import functools
import math

import jax
import jax.numpy as jnp
import numpy as np
from jax import lax
from jax.experimental import pallas as pl
from jax.experimental.pallas import tpu as pltpu
from jax.sharding import PartitionSpec as P

REACH = 3
OWN = 4
SLOTS = 16
POINTS = 64
HALF = POINTS // 2
SCREENING = 0.5
LAST_BUFFER = (2, 4, 6, 7)
BF16 = jnp.bfloat16
F32 = jnp.float32


def split_table(table):
    high = table.astype(np.float32).astype(BF16)
    low = (table - high.astype(np.float64)).astype(np.float32).astype(BF16)
    return high, low


def tables():
    modes = np.arange(POINTS, dtype=np.float64) + 1.0
    sines = np.sin(math.pi * modes[:, None] * modes[None, :] / (POINTS + 1))
    high, low = split_table(sines)
    left_x = np.concatenate([high, high, low], 1)
    none = np.zeros((POINTS, POINTS), BF16)

    def twice(block):
        return np.block([[block, none], [none, block]])

    right_z = np.concatenate([np.concatenate([twice(high), twice(low)], 1)] * 2, 0)
    even, odd = sines[:HALF, 0::2], sines[:HALF, 1::2]

    def thrice(block):
        upper, lower = split_table(block)
        return np.concatenate([upper, upper, lower], 1)

    left_y = np.concatenate([thrice(even), thrice(odd)], 0)
    back_y = np.concatenate([thrice(even.T), thrice(odd.T)], 0)
    eigen = 4.0 * np.sin(math.pi * modes / (2.0 * (POINTS + 1))) ** 2
    total = eigen[:, None, None] + eigen[None, :, None] + eigen[None, None, :] + SCREENING
    inverse = (2.0 / (POINTS + 1)) ** 3 / total
    near, far = inverse[:, :HALF], inverse[:, ::-1][:, :HALF]

    def laid(values):
        wide = np.concatenate([values, values], 2)
        return wide.astype(np.float32)

    return left_x, right_z, left_y, back_y, laid(near + far), laid(near - far)


def parts(values):
    high = values.astype(BF16)
    low = (values - high.astype(F32)).astype(BF16)
    return high, low


def dot(left, right):
    return jnp.dot(left, right, preferred_element_type=F32)


def along_first(table, values):
    high, low = parts(values)
    return dot(table, jnp.concatenate([high, low, high], 0))


def along_last(values, table):
    high, low = parts(values)
    rows = jnp.concatenate(
        [
            jnp.concatenate([high[:, :128], low[:, :128]], 1),
            jnp.concatenate([high[:, 128:], low[:, 128:]], 1),
        ],
        0,
    )
    both = dot(rows, table)
    return both[:, :128] + both[:, 128:]


UNROLL_A = 4
UNROLL_B = 8


def potential(pair, left_x, right_z, left_y, back_y, plus, minus, mixed, turned, result):
    def forward(step, carry):
        for k in range(UNROLL_A):
            c = step * UNROLL_A + k
            lanes = pl.ds(pl.multiple_of(c * 256, 256), 256)
            density = pair[0, :, lanes].astype(F32) * pair[1, :, lanes].astype(F32)
            rows = along_last(along_first(left_x[...], density), right_z[...])
            mixed[pl.ds(pl.multiple_of(c * 128, 128), 128), :] = rows
        return carry

    lax.fori_loop(0, 16 // UNROLL_A, forward, 0)

    def middle(step, carry):
        lane = lax.broadcasted_iota(jnp.int32, (HALF, 256), 1)
        first = (lane % 128) < 64
        for k in range(UNROLL_B):
            c = step * UNROLL_B + k
            x = c * 2
            taken = [mixed[pl.ds(x + s, HALF, stride=POINTS), :] for s in range(2)]
            out = along_first(left_y[...], jnp.concatenate(taken, 1))
            held = jnp.where(first, out[:HALF], out[HALF:])
            other = jnp.concatenate(
                [pltpu.roll(held[:, :128], 64, 1), pltpu.roll(held[:, 128:], 64, 1)], 1
            )
            up = jnp.concatenate([plus[x], plus[x + 1]], 1)
            down = jnp.concatenate([minus[x], minus[x + 1]], 1)
            back = along_first(back_y[...], up * held + down * other)
            kept = jnp.where(first, back[:HALF], back[HALF:])
            for s in range(2):
                turned[pl.ds(pl.multiple_of((x + s) * HALF, HALF), HALF), :] = kept[
                    :, 128 * s : 128 * s + 128
                ]
        return carry

    lax.fori_loop(0, 32 // UNROLL_B, middle, 0)

    def inverse(step, carry):
        for k in range(UNROLL_A):
            c = step * UNROLL_A + k
            taken = [turned[pl.ds(2 * c + s, POINTS, stride=HALF), :] for s in range(2)]
            rows = along_last(jnp.concatenate(taken, 1), right_z[...])
            again = jnp.concatenate([rows[:POINTS], rows[POINTS:]], 1)
            lanes = pl.ds(pl.multiple_of(c * 256, 256), 256)
            result[:, lanes] = along_first(left_x[...], again)
        return carry

    lax.fori_loop(0, 16 // UNROLL_A, inverse, 0)


def take_away(total, position, result, pair, side):
    def step(c, carry):
        lanes = pl.ds(pl.multiple_of(c * 256, 256), 256)
        total[position, :, lanes] -= result[:, lanes] * pair[side, :, lanes].astype(F32)
        return carry

    lax.fori_loop(0, 16, step, 0, unroll=4)


def list_work(phase, lists, counts, where, work):
    def row(place, found):
        back = place // SLOTS
        slot = place % SLOTS
        a = lists[back, 2 * slot]
        w = lists[back, 2 * slot + 1]
        base = (REACH - back) * OWN
        one = base + a
        two = base + w
        live = slot < counts[back]
        mine = jnp.logical_or(back == 0, w // OWN == back)
        one_at = where[one // OWN]
        two_at = where[two // OWN]

        def stage(at):
            return at // 2

        now = jnp.maximum(stage(one_at), stage(two_at)) == phase
        take = jnp.logical_and(jnp.logical_and(live, mine), now)
        work[0, found] = one
        work[1, found] = two
        return found + take.astype(jnp.int32)

    return lax.fori_loop(0, (REACH + 1) * SLOTS, row, 0)


def visit(phase, *refs):
    lists, counts, where = refs[:3]
    held = LAST_BUFFER[phase]
    buffers = refs[3 : 3 + held]
    rest = list(refs[3 + held :])
    left_x, right_z, left_y, back_y, plus, minus = rest[:6]
    rest = rest[6:]
    if phase > 0:
        before = rest.pop(0)
    total, work, pair, mixed, turned, result, sems = rest
    if phase > 0:
        total[...] = before[...]
    else:
        total[...] = jnp.zeros_like(total)
    found = list_work(phase, lists, counts, where, work)
    middle = REACH * OWN

    def fetch(item, slot):
        for side in range(2):
            position = work[side, item]
            at = where[position // OWN]
            index = position % OWN
            for b in range(held):
                @pl.when(at == b)
                def _():
                    pltpu.make_async_copy(
                        buffers[b].at[index], pair.at[slot, side], sems.at[slot, side]
                    ).start()

    @pl.when(found > 0)
    def _():
        fetch(0, 0)

    def step(item, carry):
        slot = item % 2
        for side in range(2):
            pltpu.make_async_copy(
                buffers[0].at[0], pair.at[slot, side], sems.at[slot, side]
            ).wait()

        @pl.when(item + 1 < found)
        def _():
            fetch(item + 1, 1 - slot)

        one = work[0, item]
        two = work[1, item]
        both = pair.at[slot]
        potential(
            both, left_x, right_z, left_y, back_y, plus, minus, mixed, turned, result
        )

        @pl.when(one // OWN == REACH)
        def _():
            take_away(total, one - middle, result, both, 1)

        @pl.when(jnp.logical_and(two // OWN == REACH, one != two))
        def _():
            take_away(total, two - middle, result, both, 0)

        return carry

    lax.fori_loop(0, found, step, 0)


def visit_pairs(phase, lists, counts, where, buffers, constants, before):
    smem = pl.BlockSpec(memory_space=pltpu.SMEM)
    vmem = pl.BlockSpec(memory_space=pltpu.VMEM)
    hbm = pl.BlockSpec(memory_space=pl.ANY)
    shape = (OWN, POINTS, POINTS * POINTS)
    extra = [] if before is None else [before]
    guess = (7, 8, 8, 7)[phase]
    return pl.pallas_call(
        functools.partial(visit, phase),
        out_shape=jax.ShapeDtypeStruct(shape, F32),
        in_specs=[smem] * 3 + [hbm] * len(buffers) + [vmem] * (6 + len(extra)),
        out_specs=vmem,
        scratch_shapes=[
            pltpu.SMEM((2, (REACH + 1) * SLOTS + 1), jnp.int32),
            pltpu.VMEM((2, 2, POINTS, POINTS * POINTS), BF16),
            pltpu.VMEM((POINTS * HALF, 128), F32),
            pltpu.VMEM((POINTS * HALF, 128), F32),
            pltpu.VMEM((POINTS, POINTS * POINTS), F32),
            pltpu.SemaphoreType.DMA((2, 2)),
        ],
        compiler_params=pltpu.CompilerParams(vmem_limit_bytes=40 << 20),
        cost_estimate=pl.CostEstimate(
            flops=guess * 3_000_000_000, bytes_accessed=guess << 20, transcendentals=0
        ),
        name=f"visit_{phase}",
    )(lists, counts, where, *buffers, *constants, *extra)


def moved(value, send):
    count = lax.axis_size("orb")
    return lax.ppermute(value, "orb", [(source, send(source) % count) for source in range(count)])


def swapped(value):
    return moved(value, lambda source: source ^ 1)


def shards(orbitals, pair_list, pair_counts):
    me = lax.axis_index("orb")
    even = me % 2 == 0
    row = jnp.concatenate([pair_list.reshape(-1), pair_counts])
    rows = jnp.stack(
        [row] + [moved(row, lambda source, k=k: source + k) for k in range(1, REACH + 1)]
    )
    lists = rows[:, : 2 * SLOTS]
    counts = rows[:, 2 * SLOTS]
    where = jnp.where(
        even, jnp.array([6, 3, 5, 0, 1, 2, 4], jnp.int32), jnp.array([5, 3, 1, 0, 4, 2, 6], jnp.int32)
    )
    constants = tables()

    def visited(phase, buffers, total):
        return visit_pairs(phase, lists, counts, where, buffers, constants, total)

    ahead = moved(orbitals, lambda source: source - 2)
    behind = moved(orbitals, lambda source: source + 2)
    buffers = [orbitals, swapped(orbitals)]
    total = visited(0, buffers, None)
    ahead, behind, total = lax.optimization_barrier((ahead, behind, total))
    buffers = buffers + [ahead, behind]
    beside = [swapped(ahead), swapped(behind)]
    far = moved(
        jnp.where(even, ahead, behind),
        lambda source: source - 1 if source % 2 == 0 else source + 1,
    )
    total = visited(1, buffers, total)
    buffers = buffers + beside
    total = visited(2, buffers, total)
    return visited(3, buffers + [far], total)


def solution(mesh):
    return jax.shard_map(
        shards,
        mesh=mesh,
        in_specs=(P("orb", None, None), P("orb", None), P("orb")),
        out_specs=P("orb", None, None),
        check_vma=False,
    )
```

```python
import functools
import math

import jax
import jax.numpy as jnp
import numpy as np
from jax import lax
from jax.experimental import pallas as pl
from jax.experimental.pallas import tpu as pltpu
from jax.sharding import PartitionSpec as P

REACH = 3
OWN = 4
SLOTS = 16
POINTS = 64
HALF = POINTS // 2
SCREENING = 0.5
LAST_BUFFER = (2, 3, 5, 7)
BF16 = jnp.bfloat16
F32 = jnp.float32


def split_table(table):
    high = table.astype(np.float32).astype(BF16)
    low = (table - high.astype(np.float64)).astype(np.float32).astype(BF16)
    return high, low


def tables():
    modes = np.arange(POINTS, dtype=np.float64) + 1.0
    sines = np.sin(math.pi * modes[:, None] * modes[None, :] / (POINTS + 1))
    high, low = split_table(sines)
    left_x = np.concatenate([high, high, low], 1)
    none = np.zeros((POINTS, POINTS), BF16)

    def twice(block):
        return np.block([[block, none], [none, block]])

    right_z = np.concatenate([np.concatenate([twice(high), twice(low)], 1)] * 2, 0)
    even, odd = sines[:HALF, 0::2], sines[:HALF, 1::2]

    def thrice(block):
        upper, lower = split_table(block)
        return np.concatenate([upper, upper, lower], 1)

    left_y = np.concatenate([thrice(even), thrice(odd)], 0)
    back_y = np.concatenate([thrice(even.T), thrice(odd.T)], 0)
    eigen = 4.0 * np.sin(math.pi * modes / (2.0 * (POINTS + 1))) ** 2
    total = eigen[:, None, None] + eigen[None, :, None] + eigen[None, None, :] + SCREENING
    inverse = (2.0 / (POINTS + 1)) ** 3 / total
    near, far = inverse[:, :HALF], inverse[:, ::-1][:, :HALF]

    def laid(values):
        wide = np.concatenate([values, values], 2)
        return wide.astype(np.float32)

    return left_x, right_z, left_y, back_y, laid(near + far), laid(near - far)


def parts(values):
    high = values.astype(BF16)
    low = (values - high.astype(F32)).astype(BF16)
    return high, low


def dot(left, right):
    return jnp.dot(left, right, preferred_element_type=F32)


def along_first(table, values):
    high, low = parts(values)
    return dot(table, jnp.concatenate([high, low, high], 0))


def along_last(rows, table):
    both = dot(rows, table)
    return both[:, :128] + both[:, 128:]


def side_by_side(values):
    high, low = parts(values)
    return jnp.concatenate([high, low], 1)


UNROLL_A = 16
UNROLL_Z = 8
UNROLL_B = 32
UNROLL_C = 16
PITCH_A = 72
PITCH_B = 40


def chunks(count, unroll, body):
    def step(first, carry):
        for k in range(unroll):
            body(first * unroll + k)
        return carry

    if unroll == count:
        for k in range(count):
            body(k)
    else:
        lax.fori_loop(0, count // unroll, step, 0)


def aligned(start, size):
    return pl.ds(start if isinstance(start, int) else pl.multiple_of(start, 8), size)


def lanes_of(c):
    return pl.ds(c * 256 if isinstance(c, int) else pl.multiple_of(c * 256, 256), 256)


def potential(pair, target, left_x, right_z, left_y, back_y, plus, minus, rows, mixed, turned, stacked, result, total):
    def forward_x(c):
        lanes = lanes_of(c)
        density = pair[0, :, lanes].astype(F32) * pair[1, :, lanes].astype(F32)
        high, low = parts(along_first(left_x[...], density))
        for s in range(2):
            place = aligned((2 * c + s) * POINTS, POINTS)
            rows[place, :128] = high[:, 128 * s : 128 * s + 128]
            rows[place, 128:] = low[:, 128 * s : 128 * s + 128]

    chunks(16, UNROLL_A, forward_x)

    def forward_z(c):
        out = along_last(rows[aligned(c * 256, 256), :], right_z[...])
        for s in range(4):
            mixed[aligned((4 * c + s) * PITCH_A, POINTS), :] = out[POINTS * s : POINTS * s + POINTS]

    chunks(8, UNROLL_Z, forward_z)

    lane = lax.broadcasted_iota(jnp.int32, (HALF, 256), 1)
    first = (lane % 128) < 64

    def middle(c):
        x = c * 2
        taken = [mixed[pl.ds(x + s, HALF, stride=PITCH_A), :] for s in range(2)]
        out = along_first(left_y[...], jnp.concatenate(taken, 1))
        held = jnp.where(first, out[:HALF], out[HALF:])
        other = jnp.concatenate(
            [pltpu.roll(held[:, :128], 64, 1), pltpu.roll(held[:, 128:], 64, 1)], 1
        )
        up = jnp.concatenate([plus[x], plus[x + 1]], 1)
        down = jnp.concatenate([minus[x], minus[x + 1]], 1)
        back = along_first(back_y[...], up * held + down * other)
        kept = jnp.where(first, back[:HALF], back[HALF:])
        for s in range(2):
            turned[aligned((x + s) * PITCH_B, HALF), :] = kept[:, 128 * s : 128 * s + 128]

    chunks(32, UNROLL_B, middle)

    def inverse_z(c):
        taken = [side_by_side(turned[pl.ds(4 * c + s, POINTS, stride=PITCH_B), :]) for s in range(4)]
        out = along_last(jnp.concatenate(taken, 0), right_z[...])
        high, low = parts(out)
        for s in range(4):
            lanes = pl.ds((4 * c + s) * 128 if isinstance(c, int) else pl.multiple_of((4 * c + s) * 128, 128), 128)
            stacked[:POINTS, lanes] = high[POINTS * s : POINTS * s + POINTS]
            stacked[POINTS:, lanes] = low[POINTS * s : POINTS * s + POINTS]

    chunks(8, UNROLL_Z, inverse_z)
    position, side = target

    def inverse_x(c):
        lanes = lanes_of(c)
        high, low = stacked[:POINTS, lanes], stacked[POINTS:, lanes]
        out = dot(left_x[...], jnp.concatenate([high, low, high], 0))
        result[:, lanes] = out
        total[position, :, lanes] -= out * pair[side, :, lanes].astype(F32)

    chunks(16, UNROLL_C, inverse_x)


def take_away(total, position, result, pair, side):
    def step(c, carry):
        lanes = pl.ds(pl.multiple_of(c * 256, 256), 256)
        total[position, :, lanes] -= result[:, lanes] * pair[side, :, lanes].astype(F32)
        return carry

    lax.fori_loop(0, 16, step, 0, unroll=4)


def plan(row_0, row_1, row_2, row_3, work):
    odd = lax.axis_index("orb") % 2

    def buffer_of(place):
        near = (6, 5, 3, 0, 1, 2, 4)
        far = (4, 2, 1, 0, 3, 5, 6)
        at = jnp.int32(0)
        for k in range(2 * REACH + 1):
            at = jnp.where(place == k, jnp.where(odd == 1, far[k], near[k]), at)
        return at

    for phase in range(4):
        work[8, phase] = 0
    for back, rows in enumerate((row_0, row_1, row_2, row_3)):

        def visit_row(slot, carry, back=back, rows=rows):
            a = rows[2 * slot]
            w = rows[2 * slot + 1]
            one_at = buffer_of(REACH - back)
            two_at = buffer_of(REACH - back + w // OWN)
            last = jnp.maximum(one_at, two_at)
            phase = jnp.where(last < 2, 0, jnp.where(last < 3, 1, jnp.where(last < 5, 2, 3)))
            count = work[8, phase]
            work[2 * phase, count] = one_at * OWN + a
            work[2 * phase + 1, count] = two_at * OWN + w % OWN
            if back == 0:
                work[8, phase] = count + 1
            else:
                work[8, phase] = count + (w // OWN == back).astype(jnp.int32)
            return carry

        lax.fori_loop(0, rows[2 * SLOTS], visit_row, 0)


def planned(rows):
    smem = pl.BlockSpec(memory_space=pltpu.SMEM)
    return pl.pallas_call(
        plan,
        out_shape=jax.ShapeDtypeStruct((9, (REACH + 1) * SLOTS + 1), jnp.int32),
        in_specs=[smem] * 4,
        out_specs=smem,
        name="plan",
    )(*rows)


def visit(phase, *refs):
    work = refs[0]
    held = LAST_BUFFER[phase]
    buffers = refs[1 : 1 + held]
    rest = list(refs[1 + held :])
    sources = rest[:6]
    rest = rest[6:]
    before = rest.pop(0) if phase > 0 else None
    given = rest.pop(0)
    constants = rest[:6]
    pair, rows, mixed, turned, stacked, result, sems, table_sems = rest[6:14]
    total = rest[14] if phase == 3 else given
    found = work[8, phase]

    def fetch(item, slot):
        for side in range(2):
            code = work[2 * phase + side, item]
            at = code // OWN
            index = code % OWN
            for b in range(held):
                @pl.when(at == b)
                def _():
                    pltpu.make_async_copy(
                        buffers[b].at[index], pair.at[slot, side], sems.at[slot, side]
                    ).start()

    @pl.when(found > 0)
    def _():
        fetch(0, 0)
        for k in range(6):
            pltpu.make_async_copy(sources[k], constants[k], table_sems.at[k]).start()

    if phase == 0:
        total[...] = jnp.zeros_like(total)
    if phase == 3:
        total[...] = before[...]

    @pl.when(found > 0)
    def _():
        for k in range(6):
            pltpu.make_async_copy(sources[k], constants[k], table_sems.at[k]).wait()

    def step(item, carry):
        slot = item % 2
        for side in range(2):
            pltpu.make_async_copy(
                buffers[0].at[0], pair.at[slot, side], sems.at[slot, side]
            ).wait()

        @pl.when(item + 1 < found)
        def _():
            fetch(item + 1, 1 - slot)

        one = work[2 * phase, item]
        two = work[2 * phase + 1, item]
        both = pair.at[slot]
        own_one = one < OWN
        target = jnp.where(own_one, one, two)
        side = own_one.astype(jnp.int32)
        potential(
            both, (target, side), *constants, rows, mixed, turned, stacked, result, total
        )

        @pl.when(jnp.logical_and(jnp.logical_and(own_one, two < OWN), one != two))
        def _():
            take_away(total, two, result, both, 0)

        return carry

    lax.fori_loop(0, found, step, 0)
    if phase == 3:
        copies = [
            pltpu.make_async_copy(total.at[k], given.at[k], table_sems.at[k]) for k in range(OWN)
        ]
        for copy in copies:
            copy.start()
        for copy in copies:
            copy.wait()


def visit_pairs(phase, work, buffers, constants, before):
    smem = pl.BlockSpec(memory_space=pltpu.SMEM)
    vmem = pl.BlockSpec(memory_space=pltpu.VMEM)
    anywhere = pl.BlockSpec(memory_space=pl.ANY)
    hbm = pl.BlockSpec(memory_space=pltpu.HBM)
    shape = (OWN, POINTS, POINTS * POINTS)
    extra = [] if before is None else [before]
    guess = (7, 5, 9, 9)[phase]
    return pl.pallas_call(
        functools.partial(visit, phase),
        out_shape=jax.ShapeDtypeStruct(shape, F32),
        in_specs=[smem, hbm] + [anywhere] * (len(buffers) - 1) + [hbm] * 6 + [vmem] * len(extra),
        out_specs=hbm if phase == 3 else vmem,
        scratch_shapes=[pltpu.VMEM(c.shape, c.dtype) for c in constants]
        + [
            pltpu.VMEM((2, 2, POINTS, POINTS * POINTS), BF16),
            pltpu.VMEM((POINTS * HALF, 256), BF16),
            pltpu.VMEM((HALF * PITCH_A, 128), F32),
            pltpu.VMEM((POINTS * PITCH_B, 128), F32),
            pltpu.VMEM((2 * POINTS, POINTS * POINTS), BF16),
            pltpu.VMEM((POINTS, POINTS * POINTS), F32),
            pltpu.SemaphoreType.DMA((2, 2)),
            pltpu.SemaphoreType.DMA((6,)),
        ]
        + ([pltpu.VMEM(shape, F32)] if phase == 3 else []),
        input_output_aliases={1 + len(buffers) + 6: 0} if phase in (1, 2) else {},
        compiler_params=pltpu.CompilerParams(vmem_limit_bytes=24 << 20),
        cost_estimate=pl.CostEstimate(
            flops=guess * 3_000_000_000, bytes_accessed=guess << 20, transcendentals=0
        ),
        name=f"visit_{phase}",
    )(work, *buffers, *constants, *extra)


def moved(value, send):
    count = lax.axis_size("orb")
    return lax.ppermute(value, "orb", [(source, send(source) % count) for source in range(count)])


def swapped(value):
    return moved(value, lambda source: source ^ 1)


def outward(value):
    return moved(value, lambda source: source - 2 if source % 2 == 0 else source + 2)


def onward(value):
    return moved(value, lambda source: source - 1 if source % 2 == 0 else source + 1)


def shards(orbitals, pair_list, pair_counts):
    constants = tables()
    first = outward(orbitals)
    beside = swapped(orbitals)
    row = jnp.concatenate([pair_list.reshape(-1), pair_counts])
    rows = [row] + [moved(row, lambda source, k=k: source + k) for k in range(1, REACH + 1)]
    work = planned(rows)

    def visited(phase, buffers, total):
        return visit_pairs(phase, work, buffers, constants, total)

    third = outward(beside)
    buffers = [orbitals, beside]
    total = visited(0, buffers, None)
    first, total = lax.optimization_barrier((first, total))
    first_beside = swapped(first)
    second = onward(first)
    buffers = buffers + [first]
    total = visited(1, buffers, total)
    third, total = lax.optimization_barrier((third, total))
    third_beside = swapped(third)
    buffers = buffers + [first_beside, third]
    total = visited(2, buffers, total)
    return visited(3, buffers + [third_beside, second], total)


def solution(mesh):
    return jax.shard_map(
        shards,
        mesh=mesh,
        in_specs=(P("orb", None, None), P("orb", None), P("orb")),
        out_specs=P("orb", None, None),
        check_vma=False,
    )
```

```python
import functools
import math

import jax
import jax.numpy as jnp
import numpy as np
from jax import lax
from jax.experimental import pallas as pl
from jax.experimental.pallas import tpu as pltpu
from jax.sharding import PartitionSpec as P


REACH = 3
OWN = 4
SLOTS = 16
POINTS = 64
HALF = POINTS // 2
SCREENING = 0.5
LAST_BUFFER = (2, 3, 5, 7)
CAPS = (5, 8, 8)
BF16 = jnp.bfloat16
F32 = jnp.float32


def split_table(table):
    high = table.astype(np.float32).astype(BF16)
    low = (table - high.astype(np.float64)).astype(np.float32).astype(BF16)
    return high, low


def tables():
    modes = np.arange(POINTS, dtype=np.float64) + 1.0
    sines = np.sin(math.pi * modes[:, None] * modes[None, :] / (POINTS + 1))
    high, low = split_table(sines)
    left_x = np.concatenate([high, high, low], 1)
    none = np.zeros((POINTS, POINTS), BF16)

    def twice(block):
        return np.block([[block, none], [none, block]])

    right_z = np.concatenate([np.concatenate([twice(high), twice(low)], 1)] * 2, 0)
    even, odd = sines[:HALF, 0::2], sines[:HALF, 1::2]

    def thrice(block):
        upper, lower = split_table(block)
        return np.concatenate([upper, upper, lower], 1)

    left_y = np.concatenate([thrice(even), thrice(odd)], 0)
    back_y = np.concatenate([thrice(even.T), thrice(odd.T)], 0)

    def wide(block):
        return np.pad(block, ((0, 0), (0, 256 - block.shape[1])))

    sine = np.concatenate([wide(left_x), wide(left_y), wide(back_y), right_z], 0)
    base = eigenvalues()[None, :] + eigenvalues()[:, None] + SCREENING
    base = np.concatenate([base, base], 1).astype(np.float32)
    return sine, np.stack([base[:HALF], base[::-1][:HALF]])


def eigenvalues():
    modes = np.arange(POINTS, dtype=np.float64) + 1.0
    return 4.0 * np.sin(math.pi * modes / (2.0 * (POINTS + 1))) ** 2


def parts(values):
    high = values.astype(BF16)
    low = (values - high.astype(F32)).astype(BF16)
    return high, low


def dot(left, right):
    return jnp.dot(left, right, preferred_element_type=F32)


def along_first(table, values):
    high, low = parts(values)
    return dot(table, jnp.concatenate([high, low, high], 0))


def along_last(rows, table):
    both = dot(rows, table)
    return both[:, :128] + both[:, 128:]


def side_by_side(values):
    high, low = parts(values)
    return jnp.concatenate([high, low], 1)


UNROLL_A = 16
UNROLL_Z = 8
UNROLL_B = 32
UNROLL_C = 16
PITCH_A = 72
PITCH_B = 40


def chunks(count, unroll, body):
    def step(first, carry):
        for k in range(unroll):
            body(first * unroll + k)
        return carry

    if unroll == count:
        for k in range(count):
            body(k)
    else:
        lax.fori_loop(0, count // unroll, step, 0)


def aligned(start, size):
    return pl.ds(start if isinstance(start, int) else pl.multiple_of(start, 8), size)


def lanes_of(c):
    return pl.ds(c * 256 if isinstance(c, int) else pl.multiple_of(c * 256, 256), 256)


def potential(pair, target, sine, plus, minus, rows, mixed, turned, stacked, result, total):
    left_x = sine[:POINTS, : 3 * POINTS]
    left_y = sine[POINTS : 2 * POINTS, : 3 * HALF]
    back_y = sine[2 * POINTS : 3 * POINTS, : 3 * HALF]
    right_z = sine[3 * POINTS :, :]

    def forward_x(c):
        lanes = lanes_of(c)
        density = pair[0, :, lanes].astype(F32) * pair[1, :, lanes].astype(F32)
        high, low = parts(along_first(left_x, density))
        for s in range(2):
            place = aligned((2 * c + s) * POINTS, POINTS)
            rows[place, :128] = high[:, 128 * s : 128 * s + 128]
            rows[place, 128:] = low[:, 128 * s : 128 * s + 128]

    chunks(16, UNROLL_A, forward_x)

    def forward_z(c):
        out = along_last(rows[aligned(c * 256, 256), :], right_z)
        for s in range(4):
            mixed[aligned((4 * c + s) * PITCH_A, POINTS), :] = out[POINTS * s : POINTS * s + POINTS]

    chunks(8, UNROLL_Z, forward_z)

    lane = lax.broadcasted_iota(jnp.int32, (HALF, 256), 1)
    first = (lane % 128) < 64

    def middle(c):
        x = c * 2
        taken = [mixed[pl.ds(x + s, HALF, stride=PITCH_A), :] for s in range(2)]
        out = along_first(left_y, jnp.concatenate(taken, 1))
        held = jnp.where(first, out[:HALF], out[HALF:])
        other = jnp.concatenate(
            [pltpu.roll(held[:, :128], 64, 1), pltpu.roll(held[:, 128:], 64, 1)], 1
        )
        up = jnp.concatenate([plus[x], plus[x + 1]], 1)
        down = jnp.concatenate([minus[x], minus[x + 1]], 1)
        back = along_first(back_y, up * held + down * other)
        kept = jnp.where(first, back[:HALF], back[HALF:])
        for s in range(2):
            turned[aligned((x + s) * PITCH_B, HALF), :] = kept[:, 128 * s : 128 * s + 128]

    chunks(32, UNROLL_B, middle)

    def inverse_z(c):
        taken = [side_by_side(turned[pl.ds(4 * c + s, POINTS, stride=PITCH_B), :]) for s in range(4)]
        out = along_last(jnp.concatenate(taken, 0), right_z)
        high, low = parts(out)
        for s in range(4):
            lanes = pl.ds((4 * c + s) * 128 if isinstance(c, int) else pl.multiple_of((4 * c + s) * 128, 128), 128)
            stacked[:POINTS, lanes] = high[POINTS * s : POINTS * s + POINTS]
            stacked[POINTS:, lanes] = low[POINTS * s : POINTS * s + POINTS]

    chunks(8, UNROLL_Z, inverse_z)
    position, side = target

    def inverse_x(c):
        lanes = lanes_of(c)
        high, low = stacked[:POINTS, lanes], stacked[POINTS:, lanes]
        out = dot(left_x, jnp.concatenate([high, low, high], 0))
        result[:, lanes] = out
        total[position, :, lanes] -= out * pair[side, :, lanes].astype(F32)

    chunks(16, UNROLL_C, inverse_x)


def take_away(total, position, result, pair, side):
    def step(c, carry):
        lanes = pl.ds(pl.multiple_of(c * 256, 256), 256)
        total[position, :, lanes] -= result[:, lanes] * pair[side, :, lanes].astype(F32)
        return carry

    lax.fori_loop(0, 16, step, 0, unroll=4)


def plan(row_0, row_1, row_2, row_3, base, work, plus, minus):
    for x, value in enumerate(eigenvalues()):
        scale = (2.0 / (POINTS + 1)) ** 3
        near = scale / (base[0] + np.float32(value))
        far = scale / (base[1] + np.float32(value))
        plus[x] = near + far
        minus[x] = near - far
    odd = lax.axis_index("orb") % 2

    def buffer_of(place):
        evens = (6, 5, 3, 0, 1, 2, 4)
        odds = (4, 2, 1, 0, 3, 5, 6)
        at = jnp.int32(0)
        for k in range(2 * REACH + 1):
            at = jnp.where(place == k, jnp.where(odd == 1, odds[k], evens[k]), at)
        return at

    for phase in range(4):
        work[8, phase] = 0
    for back, rows in enumerate((row_0, row_1, row_2, row_3)):

        def visit_row(slot, carry, back=back, rows=rows):
            a = rows[2 * slot]
            w = rows[2 * slot + 1]
            one_at = buffer_of(REACH - back)
            two_at = buffer_of(REACH - back + w // OWN)
            last = jnp.maximum(one_at, two_at)
            phase = jnp.where(last < 2, 0, jnp.where(last < 3, 1, jnp.where(last < 5, 2, 3)))
            for early in range(3):
                full = jnp.logical_and(phase == early, work[8, early] >= CAPS[early])
                phase = jnp.where(full, early + 1, phase)
            count = work[8, phase]
            work[2 * phase, count] = one_at * OWN + a
            work[2 * phase + 1, count] = two_at * OWN + w % OWN
            if back == 0:
                work[8, phase] = count + 1
            else:
                work[8, phase] = count + (w // OWN == back).astype(jnp.int32)
            return carry

        lax.fori_loop(0, rows[2 * SLOTS], visit_row, 0)


def planned(rows, base):
    vmem = pl.BlockSpec(memory_space=pltpu.VMEM)
    table = jax.ShapeDtypeStruct((POINTS, HALF, 128), F32)
    smem = pl.BlockSpec(memory_space=pltpu.SMEM)
    return pl.pallas_call(
        plan,
        out_shape=[jax.ShapeDtypeStruct((9, (REACH + 1) * SLOTS + 1), jnp.int32), table, table],
        in_specs=[smem] * 4 + [vmem],
        out_specs=[smem, vmem, vmem],
        name="plan",
    )(*rows, base)


def visit(phase, *refs):
    work = refs[0]
    held = LAST_BUFFER[phase]
    buffers = refs[1 : 1 + held]
    rest = list(refs[1 + held :])
    constants = rest[:3]
    rest = rest[3:]
    before = rest.pop(0) if phase > 0 else None
    given = rest.pop(0)
    pair, rows, mixed, turned, stacked, result, sems, out_sems = rest[:8]
    total = rest[8] if phase == 3 else given
    found = work[8, phase]

    def fetch(item, slot):
        for side in range(2):
            code = work[2 * phase + side, item]
            at = code // OWN
            index = code % OWN
            for b in range(held):
                @pl.when(at == b)
                def _():
                    pltpu.make_async_copy(
                        buffers[b].at[index], pair.at[slot, side], sems.at[slot, side]
                    ).start()

    @pl.when(found > 0)
    def _():
        fetch(0, 0)

    if phase == 0:
        total[...] = jnp.zeros_like(total)
    if phase == 3:
        total[...] = before[...]

    def step(item, carry):
        slot = item % 2
        for side in range(2):
            pltpu.make_async_copy(
                buffers[0].at[0], pair.at[slot, side], sems.at[slot, side]
            ).wait()

        @pl.when(item + 1 < found)
        def _():
            fetch(item + 1, 1 - slot)

        one = work[2 * phase, item]
        two = work[2 * phase + 1, item]
        both = pair.at[slot]
        own_one = one < OWN
        target = jnp.where(own_one, one, two)
        side = own_one.astype(jnp.int32)
        potential(
            both, (target, side), *constants, rows, mixed, turned, stacked, result, total
        )

        @pl.when(jnp.logical_and(jnp.logical_and(own_one, two < OWN), one != two))
        def _():
            take_away(total, two, result, both, 0)

        return carry

    lax.fori_loop(0, found, step, 0)
    if phase == 3:
        copies = [
            pltpu.make_async_copy(total.at[k], given.at[k], out_sems.at[k]) for k in range(OWN)
        ]
        for copy in copies:
            copy.start()
        for copy in copies:
            copy.wait()


def visit_pairs(phase, work, buffers, constants, before):
    smem = pl.BlockSpec(memory_space=pltpu.SMEM)
    vmem = pl.BlockSpec(memory_space=pltpu.VMEM)
    anywhere = pl.BlockSpec(memory_space=pl.ANY)
    hbm = pl.BlockSpec(memory_space=pltpu.HBM)
    shape = (OWN, POINTS, POINTS * POINTS)
    extra = [] if before is None else [before]
    guess = (7, 5, 9, 9)[phase]
    return pl.pallas_call(
        functools.partial(visit, phase),
        out_shape=jax.ShapeDtypeStruct(shape, F32),
        in_specs=[smem, hbm] + [anywhere] * (len(buffers) - 1) + [vmem] * (3 + len(extra)),
        out_specs=hbm if phase == 3 else vmem,
        scratch_shapes=[
            pltpu.VMEM((2, 2, POINTS, POINTS * POINTS), BF16),
            pltpu.VMEM((POINTS * HALF, 256), BF16),
            pltpu.VMEM((HALF * PITCH_A, 128), F32),
            pltpu.VMEM((POINTS * PITCH_B, 128), F32),
            pltpu.VMEM((2 * POINTS, POINTS * POINTS), BF16),
            pltpu.VMEM((POINTS, POINTS * POINTS), F32),
            pltpu.SemaphoreType.DMA((2, 2)),
            pltpu.SemaphoreType.DMA((OWN,)),
        ]
        + ([pltpu.VMEM(shape, F32)] if phase == 3 else []),
        input_output_aliases={1 + len(buffers) + 3: 0} if phase in (1, 2) else {},
        compiler_params=pltpu.CompilerParams(vmem_limit_bytes=24 << 20),
        cost_estimate=pl.CostEstimate(
            flops=guess * 3_000_000_000, bytes_accessed=guess << 20, transcendentals=0
        ),
    )(work, *buffers, *constants, *extra)


def moved(value, send):
    count = lax.axis_size("orb")
    return lax.ppermute(value, "orb", [(source, send(source) % count) for source in range(count)])


def swapped(value):
    return moved(value, lambda source: source ^ 1)


def outward(value):
    return moved(value, lambda source: source - 2 if source % 2 == 0 else source + 2)


def onward(value):
    return moved(value, lambda source: source - 1 if source % 2 == 0 else source + 1)


def exchange(orbitals, pair_list, pair_counts):
    sine, base = tables()
    row = jnp.concatenate([pair_list.reshape(-1), pair_counts])
    rows = [row]
    for k in range(1, REACH + 1):
        rows.append(moved(row, lambda source: source + k))
    first = outward(orbitals)
    beside = swapped(orbitals)
    work, plus, minus = planned(rows, base)
    constants = [sine, plus, minus]

    def visited(phase, buffers, total):
        return visit_pairs(phase, work, buffers, constants, total)

    third = outward(beside)
    buffers = [orbitals, beside]
    total = visited(0, buffers, None)
    first, total = lax.optimization_barrier((first, total))
    first_beside = swapped(first)
    second = onward(first)
    buffers = buffers + [first]
    total = visited(1, buffers, total)
    third, total = lax.optimization_barrier((third, total))
    third_beside = swapped(third)
    buffers = buffers + [first_beside, third]
    total = visited(2, buffers, total)
    return visited(3, buffers + [third_beside, second], total)


def solution(mesh):
    return jax.shard_map(
        exchange,
        mesh=mesh,
        in_specs=(P("orb", None, None), P("orb", None), P("orb")),
        out_specs=P("orb", None, None),
        check_vma=False,
    )
```

```python
import functools
import math

import jax
import jax.numpy as jnp
import numpy as np
from jax import lax
from jax.experimental import pallas as pl
from jax.experimental.pallas import tpu as pltpu
from jax.sharding import PartitionSpec as P


REACH = 3
OWN = 4
SLOTS = 16
POINTS = 64
HALF = POINTS // 2
SCREENING = 0.5
LAST_BUFFER = (2, 3, 5, 6, 7)
LAST = len(LAST_BUFFER) - 1
CAPS = (5, 8, 4, 5)
COUNTS = 2 * LAST + 2
BF16 = jnp.bfloat16
F32 = jnp.float32


def split_table(table):
    high = table.astype(np.float32).astype(BF16)
    low = (table - high.astype(np.float64)).astype(np.float32).astype(BF16)
    return high, low


def tables():
    modes = np.arange(POINTS, dtype=np.float64) + 1.0
    sines = np.sin(math.pi * modes[:, None] * modes[None, :] / (POINTS + 1))
    high, low = split_table(sines)
    left_x = np.concatenate([high, high, low], 1)
    none = np.zeros((POINTS, POINTS), BF16)

    def twice(block):
        return np.block([[block, none], [none, block]])

    right_z = np.concatenate([np.concatenate([twice(high), twice(low)], 1)] * 2, 0)
    even, odd = sines[:HALF, 0::2], sines[:HALF, 1::2]

    def thrice(block):
        upper, lower = split_table(block)
        return np.concatenate([upper, upper, lower], 1)

    left_y = np.concatenate([thrice(even), thrice(odd)], 0)
    back_y = np.concatenate([thrice(even.T), thrice(odd.T)], 0)

    def wide(block):
        return np.pad(block, ((0, 0), (0, 256 - block.shape[1])))

    sine = np.concatenate([wide(left_x), wide(left_y), wide(back_y), right_z], 0)
    base = eigenvalues()[None, :] + eigenvalues()[:, None] + SCREENING
    base = np.concatenate([base, base], 1).astype(np.float32)
    return sine, np.stack([base[:HALF], base[::-1][:HALF]])


def eigenvalues():
    modes = np.arange(POINTS, dtype=np.float64) + 1.0
    return 4.0 * np.sin(math.pi * modes / (2.0 * (POINTS + 1))) ** 2


def parts(values):
    high = values.astype(BF16)
    low = (values - high.astype(F32)).astype(BF16)
    return high, low


def dot(left, right):
    return jnp.dot(left, right, preferred_element_type=F32)


def along_first(table, values):
    high, low = parts(values)
    return dot(table, jnp.concatenate([high, low, high], 0))


def along_last(rows, table):
    both = dot(rows, table)
    return both[:, :128] + both[:, 128:]


def side_by_side(values):
    high, low = parts(values)
    return jnp.concatenate([high, low], 1)


UNROLL_A = 16
UNROLL_Z = 8
UNROLL_B = 32
UNROLL_C = 16
PITCH_A = 72
PITCH_B = 40


def chunks(count, unroll, body):
    def step(first, carry):
        for k in range(unroll):
            body(first * unroll + k)
        return carry

    if unroll == count:
        for k in range(count):
            body(k)
    else:
        lax.fori_loop(0, count // unroll, step, 0)


def aligned(start, size):
    return pl.ds(start if isinstance(start, int) else pl.multiple_of(start, 8), size)


def lanes_of(c):
    return pl.ds(c * 256 if isinstance(c, int) else pl.multiple_of(c * 256, 256), 256)


def potential(pair, target, sine, plus, minus, rows, mixed, turned, stacked, result, total):
    left_x = sine[:POINTS, : 3 * POINTS]
    left_y = sine[POINTS : 2 * POINTS, : 3 * HALF]
    back_y = sine[2 * POINTS : 3 * POINTS, : 3 * HALF]
    right_z = sine[3 * POINTS :, :]

    def forward_x(c):
        lanes = lanes_of(c)
        density = pair[0, :, lanes].astype(F32) * pair[1, :, lanes].astype(F32)
        high, low = parts(along_first(left_x, density))
        for s in range(2):
            place = aligned((2 * c + s) * POINTS, POINTS)
            rows[place, :128] = high[:, 128 * s : 128 * s + 128]
            rows[place, 128:] = low[:, 128 * s : 128 * s + 128]

    chunks(16, UNROLL_A, forward_x)

    def forward_z(c):
        out = along_last(rows[aligned(c * 256, 256), :], right_z)
        for s in range(4):
            mixed[aligned((4 * c + s) * PITCH_A, POINTS), :] = out[POINTS * s : POINTS * s + POINTS]

    chunks(8, UNROLL_Z, forward_z)

    lane = lax.broadcasted_iota(jnp.int32, (HALF, 256), 1)
    first = (lane % 128) < 64

    def middle(c):
        x = c * 2
        taken = [mixed[pl.ds(x + s, HALF, stride=PITCH_A), :] for s in range(2)]
        out = along_first(left_y, jnp.concatenate(taken, 1))
        held = jnp.where(first, out[:HALF], out[HALF:])
        other = jnp.concatenate(
            [pltpu.roll(held[:, :128], 64, 1), pltpu.roll(held[:, 128:], 64, 1)], 1
        )
        up = jnp.concatenate([plus[x], plus[x + 1]], 1)
        down = jnp.concatenate([minus[x], minus[x + 1]], 1)
        back = along_first(back_y, up * held + down * other)
        kept = jnp.where(first, back[:HALF], back[HALF:])
        for s in range(2):
            turned[aligned((x + s) * PITCH_B, HALF), :] = kept[:, 128 * s : 128 * s + 128]

    chunks(32, UNROLL_B, middle)

    def inverse_z(c):
        taken = [side_by_side(turned[pl.ds(4 * c + s, POINTS, stride=PITCH_B), :]) for s in range(4)]
        out = along_last(jnp.concatenate(taken, 0), right_z)
        high, low = parts(out)
        for s in range(4):
            lanes = pl.ds((4 * c + s) * 128 if isinstance(c, int) else pl.multiple_of((4 * c + s) * 128, 128), 128)
            stacked[:POINTS, lanes] = high[POINTS * s : POINTS * s + POINTS]
            stacked[POINTS:, lanes] = low[POINTS * s : POINTS * s + POINTS]

    chunks(8, UNROLL_Z, inverse_z)
    position, side = target

    def inverse_x(c):
        lanes = lanes_of(c)
        high, low = stacked[:POINTS, lanes], stacked[POINTS:, lanes]
        out = dot(left_x, jnp.concatenate([high, low, high], 0))
        result[:, lanes] = out
        total[position, :, lanes] -= out * pair[side, :, lanes].astype(F32)

    chunks(16, UNROLL_C, inverse_x)


def take_away(total, position, result, pair, side):
    def step(c, carry):
        lanes = pl.ds(pl.multiple_of(c * 256, 256), 256)
        total[position, :, lanes] -= result[:, lanes] * pair[side, :, lanes].astype(F32)
        return carry

    lax.fori_loop(0, 16, step, 0, unroll=4)


def fill_tables(base, out):
    for x, value in enumerate(eigenvalues()):
        scale = (2.0 / (POINTS + 1)) ** 3
        near = scale / (base[0] + np.float32(value))
        far = scale / (base[1] + np.float32(value))
        out[0, x] = near + far
        out[1, x] = near - far


def filled_tables(base):
    vmem = pl.BlockSpec(memory_space=pltpu.VMEM)
    return pl.pallas_call(
        fill_tables,
        out_shape=jax.ShapeDtypeStruct((2, POINTS, HALF, 128), F32),
        in_specs=[vmem],
        out_specs=vmem,
        name="fill_tables",
    )(base)


def plan(row_0, row_1, row_2, row_3, work):
    odd = lax.axis_index("orb") % 2

    def buffer_of(place):
        evens = (6, 5, 3, 0, 1, 2, 4)
        odds = (4, 2, 1, 0, 3, 5, 6)
        at = jnp.int32(0)
        for k in range(2 * REACH + 1):
            at = jnp.where(place == k, jnp.where(odd == 1, odds[k], evens[k]), at)
        return at

    for phase in range(LAST + 1):
        work[COUNTS, phase] = 0
    for back, rows in enumerate((row_0, row_1, row_2, row_3)):

        def visit_row(slot, carry, back=back, rows=rows):
            a = rows[2 * slot]
            w = rows[2 * slot + 1]
            one_at = buffer_of(REACH - back)
            two_at = buffer_of(REACH - back + w // OWN)
            last = jnp.maximum(one_at, two_at)
            phase = jnp.int32(0)
            for limit in LAST_BUFFER[:-1]:
                phase = phase + (last >= limit).astype(jnp.int32)
            for early in range(LAST):
                full = jnp.logical_and(phase == early, work[COUNTS, early] >= CAPS[early])
                phase = jnp.where(full, early + 1, phase)
            count = work[COUNTS, phase]
            work[2 * phase, count] = one_at * OWN + a
            work[2 * phase + 1, count] = two_at * OWN + w % OWN
            if back == 0:
                work[COUNTS, phase] = count + 1
            else:
                work[COUNTS, phase] = count + (w // OWN == back).astype(jnp.int32)
            return carry

        lax.fori_loop(0, rows[2 * SLOTS], visit_row, 0)


def planned(rows):
    smem = pl.BlockSpec(memory_space=pltpu.SMEM)
    return pl.pallas_call(
        plan,
        out_shape=jax.ShapeDtypeStruct((COUNTS + 1, (REACH + 1) * SLOTS + 1), jnp.int32),
        in_specs=[smem] * 4,
        out_specs=smem,
        name="plan",
    )(*rows)


def visit(phase, *refs):
    work = refs[0]
    held = LAST_BUFFER[phase]
    buffers = refs[1 : 1 + held]
    rest = list(refs[1 + held :])
    constants = [rest[0], rest[1].at[0], rest[1].at[1]]
    rest = rest[2:]
    before = rest.pop(0) if phase > 0 else None
    given = rest.pop(0)
    pair, rows, mixed, turned, stacked, result, sems, out_sems = rest[:8]
    total = rest[8] if phase == LAST else given
    found = work[COUNTS, phase]

    def fetch(item, slot):
        for side in range(2):
            code = work[2 * phase + side, item]
            at = code // OWN
            index = code % OWN
            for b in range(held):
                @pl.when(at == b)
                def _():
                    pltpu.make_async_copy(
                        buffers[b].at[index], pair.at[slot, side], sems.at[slot, side]
                    ).start()

    @pl.when(found > 0)
    def _():
        fetch(0, 0)

    if phase == 0:
        total[...] = jnp.zeros_like(total)
    if phase == LAST:
        total[...] = before[...]

    def step(item, carry):
        slot = item % 2
        for side in range(2):
            pltpu.make_async_copy(
                buffers[0].at[0], pair.at[slot, side], sems.at[slot, side]
            ).wait()

        @pl.when(item + 1 < found)
        def _():
            fetch(item + 1, 1 - slot)

        one = work[2 * phase, item]
        two = work[2 * phase + 1, item]
        both = pair.at[slot]
        own_one = one < OWN
        target = jnp.where(own_one, one, two)
        side = own_one.astype(jnp.int32)
        potential(
            both, (target, side), *constants, rows, mixed, turned, stacked, result, total
        )

        @pl.when(jnp.logical_and(jnp.logical_and(own_one, two < OWN), one != two))
        def _():
            take_away(total, two, result, both, 0)

        return carry

    lax.fori_loop(0, found, step, 0)
    if phase == LAST:
        copies = [
            pltpu.make_async_copy(total.at[k], given.at[k], out_sems.at[k]) for k in range(OWN)
        ]
        for copy in copies:
            copy.start()
        for copy in copies:
            copy.wait()


def visit_pairs(phase, work, buffers, constants, before):
    smem = pl.BlockSpec(memory_space=pltpu.SMEM)
    vmem = pl.BlockSpec(memory_space=pltpu.VMEM)
    anywhere = pl.BlockSpec(memory_space=pl.ANY)
    hbm = pl.BlockSpec(memory_space=pltpu.HBM)
    shape = (OWN, POINTS, POINTS * POINTS)
    extra = [] if before is None else [before]
    guess = (5, 8, 4, 5, 8)[phase]
    return pl.pallas_call(
        functools.partial(visit, phase),
        out_shape=jax.ShapeDtypeStruct(shape, F32),
        in_specs=[smem, hbm] + [anywhere] * (len(buffers) - 1) + [vmem] * (2 + len(extra)),
        out_specs=hbm if phase == LAST else vmem,
        scratch_shapes=[
            pltpu.VMEM((2, 2, POINTS, POINTS * POINTS), BF16),
            pltpu.VMEM((POINTS * HALF, 256), BF16),
            pltpu.VMEM((HALF * PITCH_A, 128), F32),
            pltpu.VMEM((POINTS * PITCH_B, 128), F32),
            pltpu.VMEM((2 * POINTS, POINTS * POINTS), BF16),
            pltpu.VMEM((POINTS, POINTS * POINTS), F32),
            pltpu.SemaphoreType.DMA((2, 2)),
            pltpu.SemaphoreType.DMA((OWN,)),
        ]
        + ([pltpu.VMEM(shape, F32)] if phase == LAST else []),
        input_output_aliases={1 + len(buffers) + 2: 0} if 0 < phase < LAST else {},
        compiler_params=pltpu.CompilerParams(vmem_limit_bytes=24 << 20),
        cost_estimate=pl.CostEstimate(
            flops=guess * 3_000_000_000, bytes_accessed=guess << 20, transcendentals=0
        ),
    )(work, *buffers, *constants, *extra)


def moved(value, send):
    count = lax.axis_size("orb")
    return lax.ppermute(value, "orb", [(source, send(source) % count) for source in range(count)])


def swapped(value):
    return moved(value, lambda source: source ^ 1)


def outward(value):
    return moved(value, lambda source: source - 2 if source % 2 == 0 else source + 2)


def onward(value):
    return moved(value, lambda source: source - 1 if source % 2 == 0 else source + 1)


def exchange(orbitals, pair_list, pair_counts):
    sine, base = tables()
    row = jnp.concatenate([pair_list.reshape(-1), pair_counts])
    rows = [row]
    for k in range(1, REACH + 1):
        rows.append(moved(row, lambda source: source + k))
    first = outward(orbitals)
    beside = swapped(orbitals)
    work = planned(rows)
    constants = [sine, filled_tables(base)]

    def visited(phase, buffers, total):
        return visit_pairs(phase, work, buffers, constants, total)

    third = outward(beside)
    buffers = [orbitals, beside]
    total = visited(0, buffers, None)
    first, total = lax.optimization_barrier((first, total))
    second = onward(first)
    first_beside = swapped(first)
    buffers = buffers + [first]
    total = visited(1, buffers, total)
    third, total = lax.optimization_barrier((third, total))
    third_beside = swapped(third)
    buffers = buffers + [first_beside, third]
    total = visited(2, buffers, total)
    buffers = buffers + [third_beside]
    total = visited(3, buffers, total)
    return visited(4, buffers + [second], total)


def solution(mesh):
    return jax.shard_map(
        exchange,
        mesh=mesh,
        in_specs=(P("orb", None, None), P("orb", None), P("orb")),
        out_specs=P("orb", None, None),
        check_vma=False,
    )
```

```python
import functools
import math

import jax
import jax.numpy as jnp
import numpy as np
from jax import lax
from jax.experimental import pallas as pl
from jax.experimental.pallas import tpu as pltpu
from jax.sharding import PartitionSpec as P


REACH = 3
OWN = 4
SLOTS = 16
POINTS = 64
HALF = POINTS // 2
SCREENING = 0.5
LAST_BUFFER = (2, 3, 4, 5, 6, 7)
LAST = len(LAST_BUFFER) - 1
CAPS = (5, 5, 4)
CHIP = 2 * OWN
EVENS = (6, 5, 3, 0, 1, 2, 4, 6)
ODDS = (6, 4, 2, 1, 0, 3, 5, 6)
COUNTS = 2 * LAST + 2
BF16 = jnp.bfloat16
F32 = jnp.float32


def split_table(table):
    high = table.astype(np.float32).astype(BF16)
    low = (table - high.astype(np.float64)).astype(np.float32).astype(BF16)
    return high, low


def tables():
    modes = np.arange(POINTS, dtype=np.float64) + 1.0
    sines = np.sin(math.pi * modes[:, None] * modes[None, :] / (POINTS + 1))
    high, low = split_table(sines)
    left_x = np.concatenate([high, high, low], 1)
    none = np.zeros((POINTS, POINTS), BF16)

    def twice(block):
        return np.block([[block, none], [none, block]])

    right_z = np.concatenate([np.concatenate([twice(high), twice(low)], 1)] * 2, 0)
    even, odd = sines[:HALF, 0::2], sines[:HALF, 1::2]

    def thrice(block):
        upper, lower = split_table(block)
        return np.concatenate([upper, upper, lower], 1)

    left_y = np.concatenate([thrice(even), thrice(odd)], 0)
    back_y = np.concatenate([thrice(even.T), thrice(odd.T)], 0)

    def wide(block):
        return np.pad(block, ((0, 0), (0, 256 - block.shape[1])))

    sine = np.concatenate([wide(left_x), wide(left_y), wide(back_y), right_z], 0)
    base = eigenvalues()[None, :] + eigenvalues()[:, None] + SCREENING
    base = np.concatenate([base, base], 1).astype(np.float32)
    return sine, np.stack([base[:HALF], base[::-1][:HALF]])


def eigenvalues():
    modes = np.arange(POINTS, dtype=np.float64) + 1.0
    return 4.0 * np.sin(math.pi * modes / (2.0 * (POINTS + 1))) ** 2


def parts(values):
    high = values.astype(BF16)
    low = (values - high.astype(F32)).astype(BF16)
    return high, low


def dot(left, right):
    return jnp.dot(left, right, preferred_element_type=F32)


def along_first(table, values):
    high, low = parts(values)
    return dot(table, jnp.concatenate([high, low, high], 0))


def along_last(rows, table):
    both = dot(rows, table)
    return both[:, :128] + both[:, 128:]


def side_by_side(values):
    high, low = parts(values)
    return jnp.concatenate([high, low], 1)


UNROLL_A = 16
UNROLL_Z = 8
UNROLL_B = 32
UNROLL_C = 16
PITCH_A = 72
PITCH_B = 40


def chunks(count, unroll, body):
    def step(first, carry):
        for k in range(unroll):
            body(first * unroll + k)
        return carry

    if unroll == count:
        for k in range(count):
            body(k)
    else:
        lax.fori_loop(0, count // unroll, step, 0)


def aligned(start, size):
    return pl.ds(start if isinstance(start, int) else pl.multiple_of(start, 8), size)


def lanes_of(c):
    return pl.ds(c * 256 if isinstance(c, int) else pl.multiple_of(c * 256, 256), 256)


def potential(pair, target, sine, plus, minus, rows, mixed, turned, stacked, result, total):
    left_x = sine[:POINTS, : 3 * POINTS]
    left_y = sine[POINTS : 2 * POINTS, : 3 * HALF]
    back_y = sine[2 * POINTS : 3 * POINTS, : 3 * HALF]
    right_z = sine[3 * POINTS :, :]

    def forward_x(c):
        lanes = lanes_of(c)
        density = pair[0, :, lanes].astype(F32) * pair[1, :, lanes].astype(F32)
        high, low = parts(along_first(left_x, density))
        for s in range(2):
            place = aligned((2 * c + s) * POINTS, POINTS)
            rows[place, :128] = high[:, 128 * s : 128 * s + 128]
            rows[place, 128:] = low[:, 128 * s : 128 * s + 128]

    chunks(16, UNROLL_A, forward_x)

    def forward_z(c):
        out = along_last(rows[aligned(c * 256, 256), :], right_z)
        for s in range(4):
            mixed[aligned((4 * c + s) * PITCH_A, POINTS), :] = out[POINTS * s : POINTS * s + POINTS]

    chunks(8, UNROLL_Z, forward_z)

    lane = lax.broadcasted_iota(jnp.int32, (HALF, 256), 1)
    first = (lane % 128) < 64

    def middle(c):
        x = c * 2
        taken = [mixed[pl.ds(x + s, HALF, stride=PITCH_A), :] for s in range(2)]
        out = along_first(left_y, jnp.concatenate(taken, 1))
        held = jnp.where(first, out[:HALF], out[HALF:])
        other = jnp.concatenate(
            [pltpu.roll(held[:, :128], 64, 1), pltpu.roll(held[:, 128:], 64, 1)], 1
        )
        up = jnp.concatenate([plus[x], plus[x + 1]], 1)
        down = jnp.concatenate([minus[x], minus[x + 1]], 1)
        back = along_first(back_y, up * held + down * other)
        kept = jnp.where(first, back[:HALF], back[HALF:])
        for s in range(2):
            turned[aligned((x + s) * PITCH_B, HALF), :] = kept[:, 128 * s : 128 * s + 128]

    chunks(32, UNROLL_B, middle)

    def inverse_z(c):
        taken = [side_by_side(turned[pl.ds(4 * c + s, POINTS, stride=PITCH_B), :]) for s in range(4)]
        out = along_last(jnp.concatenate(taken, 0), right_z)
        high, low = parts(out)
        for s in range(4):
            lanes = pl.ds((4 * c + s) * 128 if isinstance(c, int) else pl.multiple_of((4 * c + s) * 128, 128), 128)
            stacked[:POINTS, lanes] = high[POINTS * s : POINTS * s + POINTS]
            stacked[POINTS:, lanes] = low[POINTS * s : POINTS * s + POINTS]

    chunks(8, UNROLL_Z, inverse_z)
    position, side = target

    def inverse_x(c):
        lanes = lanes_of(c)
        high, low = stacked[:POINTS, lanes], stacked[POINTS:, lanes]
        out = dot(left_x, jnp.concatenate([high, low, high], 0))
        result[:, lanes] = out
        total[position, :, lanes] -= out * pair[side, :, lanes].astype(F32)

    chunks(16, UNROLL_C, inverse_x)


def take_away(total, position, result, pair, side):
    def step(c, carry):
        lanes = pl.ds(pl.multiple_of(c * 256, 256), 256)
        total[position, :, lanes] -= result[:, lanes] * pair[side, :, lanes].astype(F32)
        return carry

    lax.fori_loop(0, 16, step, 0, unroll=4)


def fill_tables(base, out):
    for x, value in enumerate(eigenvalues()):
        scale = (2.0 / (POINTS + 1)) ** 3
        near = scale / (base[0] + np.float32(value))
        far = scale / (base[1] + np.float32(value))
        out[0, x] = near + far
        out[1, x] = near - far


def filled_tables(base):
    vmem = pl.BlockSpec(memory_space=pltpu.VMEM)
    return pl.pallas_call(
        fill_tables,
        out_shape=jax.ShapeDtypeStruct((2, POINTS, HALF, 128), F32),
        in_specs=[vmem],
        out_specs=vmem,
        name="fill_tables",
    )(base)


def plan(own, partner, row_a, row_b, row_c, work, buffer_of):
    odd = lax.axis_index("orb") % 2
    is_odd = odd == 1
    for k in range(8):
        buffer_of[k] = jnp.where(is_odd, ODDS[k], EVENS[k])
    for phase in range(LAST + 1):
        work[COUNTS, phase] = 0

    def put(one_at, one, two_at, two, take):
        phase = jnp.maximum(jnp.maximum(one_at, two_at) - 1, 0)
        for early in range(len(CAPS)):
            full = jnp.logical_and(phase == early, work[COUNTS, early] >= CAPS[early])
            phase = jnp.where(full, early + 1, phase)
        count = work[COUNTS, phase]
        work[2 * phase, count] = one_at * OWN + one
        work[2 * phase + 1, count] = two_at * OWN + two
        work[COUNTS, phase] = count + take.astype(jnp.int32)

    turn = jnp.int32(0)
    sources = ((row_b, row_a), (row_a, row_b), (own, partner), (partner, own))
    for base, (if_even, if_odd) in enumerate(sources, 1):

        def read(at, if_even=if_even, if_odd=if_odd):
            return jnp.where(is_odd, if_odd[at], if_even[at])

        def visit_row(slot, turn, base=base, read=read):
            a = read(2 * slot)
            w = read(2 * slot + 1)
            place = base + lax.shift_right_logical(w, 2)
            if base >= REACH:
                shared = place < REACH + OWN
                mine = jnp.where(shared, turn == odd, is_odd)
            else:
                shared = jnp.logical_or(place == REACH, place == REACH + 1)
                mine = jnp.logical_and(shared, turn == odd)
            put(buffer_of[base], a, buffer_of[place], lax.bitwise_and(w, OWN - 1), mine)
            return jnp.where(shared, 1 - turn, turn)

        turn = lax.fori_loop(0, read(2 * SLOTS), visit_row, turn)

    def visit_far(slot, carry):
        w = row_c[2 * slot + 1]
        reaches = lax.shift_right_logical(w, 2) == REACH
        mine = jnp.logical_and(reaches, jnp.logical_not(is_odd))
        put(buffer_of[0], row_c[2 * slot], buffer_of[REACH], lax.bitwise_and(w, OWN - 1), mine)
        return carry

    lax.fori_loop(0, row_c[2 * SLOTS], visit_far, 0)


def planned(rows):
    smem = pl.BlockSpec(memory_space=pltpu.SMEM)
    return pl.pallas_call(
        plan,
        out_shape=jax.ShapeDtypeStruct((COUNTS + 1, 5 * SLOTS + 1), jnp.int32),
        in_specs=[smem] * 5,
        out_specs=smem,
        scratch_shapes=[pltpu.SMEM((8,), jnp.int32)],
        name="plan",
    )(*rows)


def visit(phase, *refs):
    work = refs[0]
    held = LAST_BUFFER[phase]
    buffers = refs[1 : 1 + held]
    rest = list(refs[1 + held :])
    constants = [rest[0], rest[1].at[0], rest[1].at[1]]
    rest = rest[2:]
    before = rest.pop(0) if phase > 0 else None
    given = rest.pop(0)
    pair, rows, mixed, turned, stacked, result, sems = rest[:7]
    total = given
    found = work[COUNTS, phase]

    def fetch(item, slot):
        for side in range(2):
            code = work[2 * phase + side, item]
            at = code // OWN
            index = code % OWN
            for b in range(held):
                @pl.when(at == b)
                def _():
                    pltpu.make_async_copy(
                        buffers[b].at[index], pair.at[slot, side], sems.at[slot, side]
                    ).start()

    @pl.when(found > 0)
    def _():
        fetch(0, 0)

    if phase == 0:
        total[...] = jnp.zeros_like(total)
    if phase == LAST:
        total[...] = before[:OWN]

    def step(item, carry):
        slot = item % 2
        for side in range(2):
            pltpu.make_async_copy(
                buffers[0].at[0], pair.at[slot, side], sems.at[slot, side]
            ).wait()

        @pl.when(item + 1 < found)
        def _():
            fetch(item + 1, 1 - slot)

        one = work[2 * phase, item]
        two = work[2 * phase + 1, item]
        both = pair.at[slot]
        own_one = one < CHIP
        target = jnp.where(own_one, one, two)
        side = own_one.astype(jnp.int32)
        potential(
            both, (target, side), *constants, rows, mixed, turned, stacked, result, total
        )

        @pl.when(jnp.logical_and(jnp.logical_and(own_one, two < CHIP), one != two))
        def _():
            take_away(total, two, result, both, 0)

        return carry

    lax.fori_loop(0, found, step, 0)


def visit_pairs(phase, work, buffers, constants, before):
    smem = pl.BlockSpec(memory_space=pltpu.SMEM)
    vmem = pl.BlockSpec(memory_space=pltpu.VMEM)
    anywhere = pl.BlockSpec(memory_space=pl.ANY)
    hbm = pl.BlockSpec(memory_space=pltpu.HBM)
    shape = (OWN if phase == LAST else CHIP, POINTS, POINTS * POINTS)
    extra = [] if before is None else [before]
    guess = 5
    return pl.pallas_call(
        functools.partial(visit, phase),
        out_shape=jax.ShapeDtypeStruct(shape, F32),
        in_specs=[smem, hbm] + [anywhere] * (len(buffers) - 1) + [vmem] * (2 + len(extra)),
        out_specs=vmem,
        scratch_shapes=[
            pltpu.VMEM((2, 2, POINTS, POINTS * POINTS), BF16),
            pltpu.VMEM((POINTS * HALF, 256), BF16),
            pltpu.VMEM((HALF * PITCH_A, 128), F32),
            pltpu.VMEM((POINTS * PITCH_B, 128), F32),
            pltpu.VMEM((2 * POINTS, POINTS * POINTS), BF16),
            pltpu.VMEM((POINTS, POINTS * POINTS), F32),
            pltpu.SemaphoreType.DMA((2, 2)),
        ],
        input_output_aliases={1 + len(buffers) + 2: 0} if 0 < phase < LAST else {},
        compiler_params=pltpu.CompilerParams(vmem_limit_bytes=24 << 20),
        cost_estimate=pl.CostEstimate(
            flops=guess * 3_000_000_000, bytes_accessed=guess << 20, transcendentals=0
        ),
    )(work, *buffers, *constants, *extra)


def moved(value, send):
    count = lax.axis_size("orb")
    pairs = [(source, send(source)) for source in range(count)]
    pairs = [(source, target % count) for source, target in pairs if target is not None]
    return lax.ppermute(value, "orb", pairs)


def swapped(value):
    return moved(value, lambda source: source ^ 1)


def outward(value):
    return moved(value, lambda source: source - 2 if source % 2 == 0 else source + 2)


def onward(value):
    return moved(value, lambda source: source - 1 if source % 2 == 0 else source + 1)


def exchange(orbitals, pair_list, pair_counts):
    sine, base = tables()
    row = jnp.concatenate([pair_list.reshape(-1), pair_counts])
    sends = (
        lambda source: source ^ 1,
        lambda source: source + 3 if source % 2 == 0 else source + 1,
        lambda source: source + 2,
        lambda source: source + 3 if source % 2 == 1 else None,
    )
    rows = [row]
    for send in sends:
        rows.append(moved(row, send))
    first = outward(orbitals)
    beside = swapped(orbitals)
    work = planned(rows)
    constants = [sine, filled_tables(base)]

    def visited(phase, buffers, total):
        return visit_pairs(phase, work, buffers, constants, total)

    third = outward(beside)
    buffers = [orbitals, beside]
    total = visited(0, buffers, None)
    first, total = lax.optimization_barrier((first, total))
    second = onward(first)
    first_beside = swapped(first)
    buffers = buffers + [first]
    total = visited(1, buffers, total)
    buffers = buffers + [first_beside]
    total = visited(2, buffers, total)
    third, total = lax.optimization_barrier((third, total))
    third_beside = swapped(third)
    buffers = buffers + [third]
    total = visited(3, buffers, total)
    buffers = buffers + [third_beside]
    total = visited(4, buffers, total)
    given = swapped(total[OWN:])
    return visited(5, buffers + [second], total) + given


def solution(mesh):
    return jax.shard_map(
        exchange,
        mesh=mesh,
        in_specs=(P("orb", None, None), P("orb", None), P("orb")),
        out_specs=P("orb", None, None),
        check_vma=False,
    )
```

```python
import functools
import math

import jax
import jax.numpy as jnp
import numpy as np
from jax import lax
from jax.experimental import pallas as pl
from jax.experimental.pallas import tpu as pltpu
from jax.sharding import PartitionSpec as P


REACH = 3
OWN = 4
SLOTS = 16
POINTS = 64
HALF = POINTS // 2
SCREENING = 0.5
LAST_BUFFER = (2, 3, 4, 5, 6, 7)
LAST = len(LAST_BUFFER) - 1
CAPS = (5, 5, 4)
CHIP = 2 * OWN
LENGTH = 2 * SLOTS + 1
EVENS = (6, 5, 3, 0, 1, 2, 4, 6)
ODDS = (6, 4, 2, 1, 0, 3, 5, 6)
COUNTS = 2 * LAST + 2
BF16 = jnp.bfloat16
F32 = jnp.float32


def split_table(table):
    high = table.astype(np.float32).astype(BF16)
    low = (table - high.astype(np.float64)).astype(np.float32).astype(BF16)
    return high, low


def tables():
    modes = np.arange(POINTS, dtype=np.float64) + 1.0
    sines = np.sin(math.pi * modes[:, None] * modes[None, :] / (POINTS + 1))
    high, low = split_table(sines)
    left_x = np.concatenate([high, high, low], 1)
    none = np.zeros((POINTS, POINTS), BF16)

    def twice(block):
        return np.block([[block, none], [none, block]])

    right_z = np.concatenate([np.concatenate([twice(high), twice(low)], 1)] * 2, 0)
    even, odd = sines[:HALF, 0::2], sines[:HALF, 1::2]

    def thrice(block):
        upper, lower = split_table(block)
        return np.concatenate([upper, upper, lower], 1)

    left_y = np.concatenate([thrice(even), thrice(odd)], 0)
    back_y = np.concatenate([thrice(even.T), thrice(odd.T)], 0)

    def wide(block):
        return np.pad(block, ((0, 0), (0, 256 - block.shape[1])))

    sine = np.concatenate([wide(left_x), wide(left_y), wide(back_y), right_z], 0)
    base = eigenvalues()[None, :] + eigenvalues()[:, None] + SCREENING
    base = np.concatenate([base, base], 1).astype(np.float32)
    return sine, np.stack([base[:HALF], base[::-1][:HALF]])


def eigenvalues():
    modes = np.arange(POINTS, dtype=np.float64) + 1.0
    return 4.0 * np.sin(math.pi * modes / (2.0 * (POINTS + 1))) ** 2


def parts(values):
    high = values.astype(BF16)
    low = (values - high.astype(F32)).astype(BF16)
    return high, low


def dot(left, right):
    return jnp.dot(left, right, preferred_element_type=F32)


def along_first(table, values):
    high, low = parts(values)
    return dot(table, jnp.concatenate([high, low, high], 0))


def along_last(rows, table):
    both = dot(rows, table)
    return both[:, :128] + both[:, 128:]


def side_by_side(values):
    high, low = parts(values)
    return jnp.concatenate([high, low], 1)


UNROLL_A = 16
UNROLL_Z = 8
UNROLL_B = 32
UNROLL_C = 16
PITCH_A = 72
PITCH_B = 40


def chunks(count, unroll, body):
    def step(first, carry):
        for k in range(unroll):
            body(first * unroll + k)
        return carry

    if unroll == count:
        for k in range(count):
            body(k)
    else:
        lax.fori_loop(0, count // unroll, step, 0)


def aligned(start, size):
    return pl.ds(start if isinstance(start, int) else pl.multiple_of(start, 8), size)


def lanes_of(c):
    return pl.ds(c * 256 if isinstance(c, int) else pl.multiple_of(c * 256, 256), 256)


def potential(pair, target, sine, plus, minus, rows, mixed, turned, stacked, result, total):
    left_x = sine[:POINTS, : 3 * POINTS]
    left_y = sine[POINTS : 2 * POINTS, : 3 * HALF]
    back_y = sine[2 * POINTS : 3 * POINTS, : 3 * HALF]
    right_z = sine[3 * POINTS :, :]

    def forward_x(c):
        lanes = lanes_of(c)
        density = pair[0, :, lanes].astype(F32) * pair[1, :, lanes].astype(F32)
        high, low = parts(along_first(left_x, density))
        for s in range(2):
            place = aligned((2 * c + s) * POINTS, POINTS)
            rows[place, :128] = high[:, 128 * s : 128 * s + 128]
            rows[place, 128:] = low[:, 128 * s : 128 * s + 128]

    chunks(16, UNROLL_A, forward_x)

    def forward_z(c):
        out = along_last(rows[aligned(c * 256, 256), :], right_z)
        for s in range(4):
            mixed[aligned((4 * c + s) * PITCH_A, POINTS), :] = out[POINTS * s : POINTS * s + POINTS]

    chunks(8, UNROLL_Z, forward_z)

    lane = lax.broadcasted_iota(jnp.int32, (HALF, 256), 1)
    first = (lane % 128) < 64

    def middle(c):
        x = c * 2
        taken = [mixed[pl.ds(x + s, HALF, stride=PITCH_A), :] for s in range(2)]
        out = along_first(left_y, jnp.concatenate(taken, 1))
        held = jnp.where(first, out[:HALF], out[HALF:])
        other = jnp.concatenate(
            [pltpu.roll(held[:, :128], 64, 1), pltpu.roll(held[:, 128:], 64, 1)], 1
        )
        up = jnp.concatenate([plus[x], plus[x + 1]], 1)
        down = jnp.concatenate([minus[x], minus[x + 1]], 1)
        back = along_first(back_y, up * held + down * other)
        kept = jnp.where(first, back[:HALF], back[HALF:])
        for s in range(2):
            turned[aligned((x + s) * PITCH_B, HALF), :] = kept[:, 128 * s : 128 * s + 128]

    chunks(32, UNROLL_B, middle)

    def inverse_z(c):
        taken = [side_by_side(turned[pl.ds(4 * c + s, POINTS, stride=PITCH_B), :]) for s in range(4)]
        out = along_last(jnp.concatenate(taken, 0), right_z)
        high, low = parts(out)
        for s in range(4):
            lanes = pl.ds((4 * c + s) * 128 if isinstance(c, int) else pl.multiple_of((4 * c + s) * 128, 128), 128)
            stacked[:POINTS, lanes] = high[POINTS * s : POINTS * s + POINTS]
            stacked[POINTS:, lanes] = low[POINTS * s : POINTS * s + POINTS]

    chunks(8, UNROLL_Z, inverse_z)
    position, side = target

    def inverse_x(c):
        lanes = lanes_of(c)
        high, low = stacked[:POINTS, lanes], stacked[POINTS:, lanes]
        out = dot(left_x, jnp.concatenate([high, low, high], 0))
        result[:, lanes] = out
        total[position, :, lanes] -= out * pair[side, :, lanes].astype(F32)

    chunks(16, UNROLL_C, inverse_x)


def take_away(total, position, result, pair, side):
    def step(c, carry):
        lanes = pl.ds(pl.multiple_of(c * 256, 256), 256)
        total[position, :, lanes] -= result[:, lanes] * pair[side, :, lanes].astype(F32)
        return carry

    lax.fori_loop(0, 16, step, 0, unroll=4)


def fill_tables(base, out):
    for x, value in enumerate(eigenvalues()):
        scale = (2.0 / (POINTS + 1)) ** 3
        near = scale / (base[0] + np.float32(value))
        far = scale / (base[1] + np.float32(value))
        out[0, x] = near + far
        out[1, x] = near - far


def filled_tables(base):
    vmem = pl.BlockSpec(memory_space=pltpu.VMEM)
    return pl.pallas_call(
        fill_tables,
        out_shape=jax.ShapeDtypeStruct((2, POINTS, HALF, 128), F32),
        in_specs=[vmem],
        out_specs=vmem,
        name="fill_tables",
    )(base)


def plan(own, partner, for_even, for_odd, far_rows, work, buffer_of):
    odd = lax.axis_index("orb") % 2
    is_odd = odd == 1
    for k in range(8):
        buffer_of[k] = jnp.where(is_odd, ODDS[k], EVENS[k])
    for phase in range(LAST + 1):
        work[COUNTS, phase] = 0

    def put(one_at, one, two_at, two, take):
        phase = jnp.maximum(jnp.maximum(one_at, two_at) - 1, 0)
        for early in range(len(CAPS)):
            full = jnp.logical_and(phase == early, work[COUNTS, early] >= CAPS[early])
            phase = jnp.where(full, early + 1, phase)
        count = work[COUNTS, phase]
        work[2 * phase, count] = one_at * OWN + one
        work[2 * phase + 1, count] = two_at * OWN + two
        work[COUNTS, phase] = count + take.astype(jnp.int32)

    turn = jnp.int32(0)
    sources = (
        (for_even, for_odd, 0),
        (for_even, for_odd, LENGTH),
        (own, partner, 0),
        (partner, own, 0),
    )
    for base, (if_even, if_odd, begin) in enumerate(sources, 1):

        def read(at, if_even=if_even, if_odd=if_odd, begin=begin):
            return jnp.where(is_odd, if_odd[begin + at], if_even[begin + at])

        def visit_row(slot, turn, base=base, read=read):
            a = read(2 * slot)
            w = read(2 * slot + 1)
            place = base + lax.shift_right_logical(w, 2)
            if base >= REACH:
                shared = place < REACH + OWN
                mine = jnp.where(shared, turn == odd, is_odd)
            else:
                shared = jnp.logical_or(place == REACH, place == REACH + 1)
                mine = jnp.logical_and(shared, turn == odd)
            put(buffer_of[base], a, buffer_of[place], lax.bitwise_and(w, OWN - 1), mine)
            return jnp.where(shared, 1 - turn, turn)

        turn = lax.fori_loop(0, read(2 * SLOTS), visit_row, turn)

    def visit_far(slot, carry):
        w = far_rows[LENGTH + 2 * slot + 1]
        reaches = lax.shift_right_logical(w, 2) == REACH
        mine = jnp.logical_and(reaches, jnp.logical_not(is_odd))
        put(buffer_of[0], far_rows[LENGTH + 2 * slot], buffer_of[REACH], lax.bitwise_and(w, OWN - 1), mine)
        return carry

    lax.fori_loop(0, far_rows[LENGTH + 2 * SLOTS], visit_far, 0)


def planned(rows):
    smem = pl.BlockSpec(memory_space=pltpu.SMEM)
    return pl.pallas_call(
        plan,
        out_shape=jax.ShapeDtypeStruct((COUNTS + 1, 5 * SLOTS + 1), jnp.int32),
        in_specs=[smem] * 5,
        out_specs=smem,
        scratch_shapes=[pltpu.SMEM((8,), jnp.int32)],
        name="plan",
    )(*rows)


def visit(phase, *refs):
    work = refs[0]
    held = LAST_BUFFER[phase]
    buffers = refs[1 : 1 + held]
    rest = list(refs[1 + held :])
    constants = [rest[0], rest[1].at[0], rest[1].at[1]]
    rest = rest[2:]
    before = rest.pop(0) if phase > 0 else None
    given = rest.pop(0)
    pair, rows, mixed, turned, stacked, result, sems = rest[:7]
    total = given
    found = work[COUNTS, phase]

    def fetch(item, slot):
        for side in range(2):
            code = work[2 * phase + side, item]
            at = code // OWN
            index = code % OWN
            for b in range(held):
                @pl.when(at == b)
                def _():
                    pltpu.make_async_copy(
                        buffers[b].at[index], pair.at[slot, side], sems.at[slot, side]
                    ).start()

    @pl.when(found > 0)
    def _():
        fetch(0, 0)

    if phase == 0:
        total[...] = jnp.zeros_like(total)
    if phase == LAST:
        total[...] = before[:OWN]

    def step(item, carry):
        slot = item % 2
        for side in range(2):
            pltpu.make_async_copy(
                buffers[0].at[0], pair.at[slot, side], sems.at[slot, side]
            ).wait()

        @pl.when(item + 1 < found)
        def _():
            fetch(item + 1, 1 - slot)

        one = work[2 * phase, item]
        two = work[2 * phase + 1, item]
        both = pair.at[slot]
        own_one = one < CHIP
        target = jnp.where(own_one, one, two)
        side = own_one.astype(jnp.int32)
        potential(
            both, (target, side), *constants, rows, mixed, turned, stacked, result, total
        )

        @pl.when(jnp.logical_and(jnp.logical_and(own_one, two < CHIP), one != two))
        def _():
            take_away(total, two, result, both, 0)

        return carry

    lax.fori_loop(0, found, step, 0)


def visit_pairs(phase, work, buffers, constants, before):
    smem = pl.BlockSpec(memory_space=pltpu.SMEM)
    vmem = pl.BlockSpec(memory_space=pltpu.VMEM)
    anywhere = pl.BlockSpec(memory_space=pl.ANY)
    hbm = pl.BlockSpec(memory_space=pltpu.HBM)
    shape = (OWN if phase == LAST else CHIP, POINTS, POINTS * POINTS)
    extra = [] if before is None else [before]
    guess = 5
    return pl.pallas_call(
        functools.partial(visit, phase),
        out_shape=jax.ShapeDtypeStruct(shape, F32),
        in_specs=[smem, hbm] + [anywhere] * (len(buffers) - 1) + [vmem] * (2 + len(extra)),
        out_specs=vmem,
        scratch_shapes=[
            pltpu.VMEM((2, 2, POINTS, POINTS * POINTS), BF16),
            pltpu.VMEM((POINTS * HALF, 256), BF16),
            pltpu.VMEM((HALF * PITCH_A, 128), F32),
            pltpu.VMEM((POINTS * PITCH_B, 128), F32),
            pltpu.VMEM((2 * POINTS, POINTS * POINTS), BF16),
            pltpu.VMEM((POINTS, POINTS * POINTS), F32),
            pltpu.SemaphoreType.DMA((2, 2)),
        ],
        input_output_aliases={1 + len(buffers) + 2: 0} if 0 < phase < LAST else {},
        compiler_params=pltpu.CompilerParams(vmem_limit_bytes=24 << 20),
        cost_estimate=pl.CostEstimate(
            flops=guess * 3_000_000_000, bytes_accessed=guess << 20, transcendentals=0
        ),
    )(work, *buffers, *constants, *extra)


def moved(value, send):
    count = lax.axis_size("orb")
    pairs = [(source, send(source)) for source in range(count)]
    pairs = [(source, target % count) for source, target in pairs if target is not None]
    return lax.ppermute(value, "orb", pairs)


def swapped(value):
    return moved(value, lambda source: source ^ 1)


def outward(value):
    return moved(value, lambda source: source - 2 if source % 2 == 0 else source + 2)


def onward(value):
    return moved(value, lambda source: source - 1 if source % 2 == 0 else source + 1)


def exchange(orbitals, pair_list, pair_counts):
    sine, base = tables()
    first = outward(orbitals)
    row = jnp.concatenate([pair_list.reshape(-1), pair_counts])
    partner = swapped(row)
    beside = swapped(orbitals)
    chip_rows = jnp.concatenate([row, partner])
    rows = [row, partner]
    for k in range(2, 5):
        rows.append(moved(chip_rows, lambda source: source + k if source % 2 == 0 else None))
    work = planned(rows)
    constants = [sine, filled_tables(base)]

    def visited(phase, buffers, total):
        return visit_pairs(phase, work, buffers, constants, total)

    third = outward(beside)
    buffers = [orbitals, beside]
    total = visited(0, buffers, None)
    first, total = lax.optimization_barrier((first, total))
    second = onward(first)
    first_beside = swapped(first)
    buffers = buffers + [first]
    total = visited(1, buffers, total)
    buffers = buffers + [first_beside]
    total = visited(2, buffers, total)
    third, total = lax.optimization_barrier((third, total))
    third_beside = swapped(third)
    buffers = buffers + [third]
    total = visited(3, buffers, total)
    buffers = buffers + [third_beside]
    total = visited(4, buffers, total)
    given = swapped(total[OWN:])
    return visited(5, buffers + [second], total) + given


def solution(mesh):
    return jax.shard_map(
        exchange,
        mesh=mesh,
        in_specs=(P("orb", None, None), P("orb", None), P("orb")),
        out_specs=P("orb", None, None),
        check_vma=False,
    )
```

```python
import functools
import math

import jax
import jax.numpy as jnp
import numpy as np
from jax import lax
from jax.experimental import pallas as pl
from jax.experimental.pallas import tpu as pltpu
from jax.sharding import PartitionSpec as P


REACH = 3
OWN = 4
SLOTS = 16
POINTS = 64
HALF = POINTS // 2
SCREENING = 0.5
LAST_BUFFER = (2, 3, 4, 5, 6, 7)
LAST = len(LAST_BUFFER) - 1
CAPS = (5, 5, 4)
CHIP = 2 * OWN
EVENS = (6, 5, 3, 0, 1, 2, 4, 6)
ODDS = (6, 4, 2, 1, 0, 3, 5, 6)
COUNTS = 2 * LAST + 2
BF16 = jnp.bfloat16
F32 = jnp.float32


def split_table(table):
    high = table.astype(np.float32).astype(BF16)
    low = (table - high.astype(np.float64)).astype(np.float32).astype(BF16)
    return high, low


def tables():
    modes = np.arange(POINTS, dtype=np.float64) + 1.0
    sines = np.sin(math.pi * modes[:, None] * modes[None, :] / (POINTS + 1))
    high, low = split_table(sines)
    left_x = np.concatenate([high, high, low], 1)
    none = np.zeros((POINTS, POINTS), BF16)

    def twice(block):
        return np.block([[block, none], [none, block]])

    right_z = np.concatenate([np.concatenate([twice(high), twice(low)], 1)] * 2, 0)
    even, odd = sines[:HALF, 0::2], sines[:HALF, 1::2]

    def thrice(block):
        upper, lower = split_table(block)
        return np.concatenate([upper, upper, lower], 1)

    left_y = np.concatenate([thrice(even), thrice(odd)], 0)
    back_y = np.concatenate([thrice(even.T), thrice(odd.T)], 0)

    def wide(block):
        return np.pad(block, ((0, 0), (0, 256 - block.shape[1])))

    sine = np.concatenate([wide(left_x), wide(left_y), wide(back_y), right_z], 0)
    base = eigenvalues()[None, :] + eigenvalues()[:, None] + SCREENING
    base = np.concatenate([base, base], 1).astype(np.float32)
    return sine, np.stack([base[:HALF], base[::-1][:HALF]])


def eigenvalues():
    modes = np.arange(POINTS, dtype=np.float64) + 1.0
    return 4.0 * np.sin(math.pi * modes / (2.0 * (POINTS + 1))) ** 2


def parts(values):
    high = values.astype(BF16)
    low = (values - high.astype(F32)).astype(BF16)
    return high, low


def dot(left, right):
    return jnp.dot(left, right, preferred_element_type=F32)


def along_first(table, values):
    high, low = parts(values)
    return dot(table, jnp.concatenate([high, low, high], 0))


def along_last(rows, table):
    both = dot(rows, table)
    return both[:, :128] + both[:, 128:]


def side_by_side(values):
    high, low = parts(values)
    return jnp.concatenate([high, low], 1)


UNROLL_A = 16
UNROLL_Z = 8
UNROLL_B = 32
UNROLL_C = 16
PITCH_A = 72
PITCH_B = 40


def chunks(count, unroll, body):
    def step(first, carry):
        for k in range(unroll):
            body(first * unroll + k)
        return carry

    if unroll == count:
        for k in range(count):
            body(k)
    else:
        lax.fori_loop(0, count // unroll, step, 0)


def aligned(start, size):
    return pl.ds(start if isinstance(start, int) else pl.multiple_of(start, 8), size)


def lanes_of(c):
    return pl.ds(c * 256 if isinstance(c, int) else pl.multiple_of(c * 256, 256), 256)


def potential(pair, target, sine, plus, minus, rows, mixed, turned, stacked, result, total):
    left_x = sine[:POINTS, : 3 * POINTS]
    left_y = sine[POINTS : 2 * POINTS, : 3 * HALF]
    back_y = sine[2 * POINTS : 3 * POINTS, : 3 * HALF]
    right_z = sine[3 * POINTS :, :]

    def forward_x(c):
        lanes = lanes_of(c)
        density = pair[0, :, lanes].astype(F32) * pair[1, :, lanes].astype(F32)
        high, low = parts(along_first(left_x, density))
        for s in range(2):
            place = aligned((2 * c + s) * POINTS, POINTS)
            rows[place, :128] = high[:, 128 * s : 128 * s + 128]
            rows[place, 128:] = low[:, 128 * s : 128 * s + 128]

    chunks(16, UNROLL_A, forward_x)

    def forward_z(c):
        out = along_last(rows[aligned(c * 256, 256), :], right_z)
        for s in range(4):
            mixed[aligned((4 * c + s) * PITCH_A, POINTS), :] = out[POINTS * s : POINTS * s + POINTS]

    chunks(8, UNROLL_Z, forward_z)

    lane = lax.broadcasted_iota(jnp.int32, (HALF, 256), 1)
    first = (lane % 128) < 64

    def middle(c):
        x = c * 2
        taken = [mixed[pl.ds(x + s, HALF, stride=PITCH_A), :] for s in range(2)]
        out = along_first(left_y, jnp.concatenate(taken, 1))
        held = jnp.where(first, out[:HALF], out[HALF:])
        other = jnp.concatenate(
            [pltpu.roll(held[:, :128], 64, 1), pltpu.roll(held[:, 128:], 64, 1)], 1
        )
        up = jnp.concatenate([plus[x], plus[x + 1]], 1)
        down = jnp.concatenate([minus[x], minus[x + 1]], 1)
        back = along_first(back_y, up * held + down * other)
        kept = jnp.where(first, back[:HALF], back[HALF:])
        for s in range(2):
            turned[aligned((x + s) * PITCH_B, HALF), :] = kept[:, 128 * s : 128 * s + 128]

    chunks(32, UNROLL_B, middle)

    def inverse_z(c):
        taken = [side_by_side(turned[pl.ds(4 * c + s, POINTS, stride=PITCH_B), :]) for s in range(4)]
        out = along_last(jnp.concatenate(taken, 0), right_z)
        high, low = parts(out)
        for s in range(4):
            lanes = pl.ds((4 * c + s) * 128 if isinstance(c, int) else pl.multiple_of((4 * c + s) * 128, 128), 128)
            stacked[:POINTS, lanes] = high[POINTS * s : POINTS * s + POINTS]
            stacked[POINTS:, lanes] = low[POINTS * s : POINTS * s + POINTS]

    chunks(8, UNROLL_Z, inverse_z)
    position, side = target

    def inverse_x(c):
        lanes = lanes_of(c)
        high, low = stacked[:POINTS, lanes], stacked[POINTS:, lanes]
        out = dot(left_x, jnp.concatenate([high, low, high], 0))
        result[:, lanes] = out
        total[position, :, lanes] -= out * pair[side, :, lanes].astype(F32)

    chunks(16, UNROLL_C, inverse_x)


def take_away(total, position, result, pair, side):
    def step(c, carry):
        lanes = pl.ds(pl.multiple_of(c * 256, 256), 256)
        total[position, :, lanes] -= result[:, lanes] * pair[side, :, lanes].astype(F32)
        return carry

    lax.fori_loop(0, 16, step, 0, unroll=4)


def fill_tables(base, out):
    for x, value in enumerate(eigenvalues()):
        scale = (2.0 / (POINTS + 1)) ** 3
        near = scale / (base[0] + np.float32(value))
        far = scale / (base[1] + np.float32(value))
        out[0, x] = near + far
        out[1, x] = near - far


def filled_tables(base):
    vmem = pl.BlockSpec(memory_space=pltpu.VMEM)
    return pl.pallas_call(
        fill_tables,
        out_shape=jax.ShapeDtypeStruct((2, POINTS, HALF, 128), F32),
        in_specs=[vmem],
        out_specs=vmem,
        name="fill_tables",
    )(base)


def share(row, out, send_sems, recv_sems, own_sem):
    me = lax.axis_index("orb")
    count = lax.axis_size("orb")
    odd = me % 2
    targets = [me + 1 - 2 * odd, me + 2, me + 3 - 2 * odd, me + 5 - 2 * odd]
    sources = [me + 1 - 2 * odd, me - 2, me - 1 - 2 * odd, me - 3 - 2 * odd]
    targets = [lax.rem(target + count, count) for target in targets]
    sources = [lax.rem(source + count, count) for source in sources]
    barrier = pltpu.get_barrier_semaphore()
    for source in sources:
        pl.semaphore_signal(
            barrier, inc=1, device_id=(source,), device_id_type=pl.DeviceIdType.MESH
        )
    pl.semaphore_wait(barrier, 4)
    copies = [pltpu.make_async_copy(row, out.at[4], own_sem)]
    for k, target in enumerate(targets):
        copies.append(
            pltpu.make_async_remote_copy(
                src_ref=row,
                dst_ref=out.at[k],
                send_sem=send_sems.at[k],
                recv_sem=recv_sems.at[k],
                device_id=(target,),
                device_id_type=pl.DeviceIdType.MESH,
            )
        )
    for copy in copies:
        copy.start()
    for copy in copies:
        copy.wait()


def shared(row):
    vmem = pl.BlockSpec(memory_space=pltpu.VMEM)
    return pl.pallas_call(
        share,
        out_shape=jax.ShapeDtypeStruct((5, 1, 128), jnp.int32),
        in_specs=[vmem],
        out_specs=vmem,
        scratch_shapes=[
            pltpu.SemaphoreType.DMA((4,)),
            pltpu.SemaphoreType.DMA((4,)),
            pltpu.SemaphoreType.DMA,
        ],
        compiler_params=pltpu.CompilerParams(collective_id=0, has_side_effects=True),
        name="share",
    )(row)


def plan(rows, work, buffer_of):
    odd = lax.axis_index("orb") % 2
    is_odd = odd == 1
    for k in range(8):
        buffer_of[k] = jnp.where(is_odd, ODDS[k], EVENS[k])
    for phase in range(LAST + 1):
        work[COUNTS, phase] = 0

    def put(one_at, one, two_at, two, take):
        phase = jnp.maximum(jnp.maximum(one_at, two_at) - 1, 0)
        for early in range(len(CAPS)):
            full = jnp.logical_and(phase == early, work[COUNTS, early] >= CAPS[early])
            phase = jnp.where(full, early + 1, phase)
        count = work[COUNTS, phase]
        work[2 * phase, count] = one_at * OWN + one
        work[2 * phase + 1, count] = two_at * OWN + two
        work[COUNTS, phase] = count + take.astype(jnp.int32)

    turn = jnp.int32(0)
    sources = ((1, 2), (2, 1), (4, 0), (0, 4))
    for base, (if_even, if_odd) in enumerate(sources, 1):
        which = jnp.where(is_odd, if_odd, if_even)

        def read(at, which=which):
            return rows[which, 0, at]

        def visit_row(slot, turn, base=base, read=read):
            a = read(2 * slot)
            w = read(2 * slot + 1)
            place = base + lax.shift_right_logical(w, 2)
            if base >= REACH:
                shared = place < REACH + OWN
                mine = jnp.where(shared, turn == odd, is_odd)
            else:
                shared = jnp.logical_or(place == REACH, place == REACH + 1)
                mine = jnp.logical_and(shared, turn == odd)
            put(buffer_of[base], a, buffer_of[place], lax.bitwise_and(w, OWN - 1), mine)
            return jnp.where(shared, 1 - turn, turn)

        turn = lax.fori_loop(0, read(2 * SLOTS), visit_row, turn)

    def visit_far(slot, carry):
        w = rows[3, 0, 2 * slot + 1]
        reaches = lax.shift_right_logical(w, 2) == REACH
        index = lax.bitwise_and(w, OWN - 1)
        put(buffer_of[0], rows[3, 0, 2 * slot], buffer_of[REACH], index, reaches)
        return carry

    lax.fori_loop(0, jnp.where(is_odd, 0, rows[3, 0, 2 * SLOTS]), visit_far, 0)


def planned(rows):
    smem = pl.BlockSpec(memory_space=pltpu.SMEM)
    return pl.pallas_call(
        plan,
        out_shape=jax.ShapeDtypeStruct((COUNTS + 1, 5 * SLOTS + 1), jnp.int32),
        in_specs=[smem],
        out_specs=smem,
        scratch_shapes=[pltpu.SMEM((8,), jnp.int32)],
        name="plan",
    )(rows)


def visit(phase, *refs):
    work = refs[0]
    held = LAST_BUFFER[phase]
    buffers = refs[1 : 1 + held]
    rest = list(refs[1 + held :])
    constants = [rest[0], rest[1].at[0], rest[1].at[1]]
    rest = rest[2:]
    before = rest.pop(0) if phase > 0 else None
    given = rest.pop(0)
    pair, rows, mixed, turned, stacked, result, sems = rest[:7]
    total = given
    found = work[COUNTS, phase]

    def fetch(item, slot):
        for side in range(2):
            code = work[2 * phase + side, item]
            at = code // OWN
            index = code % OWN
            for b in range(held):
                @pl.when(at == b)
                def _():
                    pltpu.make_async_copy(
                        buffers[b].at[index], pair.at[slot, side], sems.at[slot, side]
                    ).start()

    @pl.when(found > 0)
    def _():
        fetch(0, 0)

    if phase == 0:
        total[...] = jnp.zeros_like(total)
    if phase == LAST:
        total[...] = before[:OWN]

    def step(item, carry):
        slot = item % 2
        for side in range(2):
            pltpu.make_async_copy(
                buffers[0].at[0], pair.at[slot, side], sems.at[slot, side]
            ).wait()

        @pl.when(item + 1 < found)
        def _():
            fetch(item + 1, 1 - slot)

        one = work[2 * phase, item]
        two = work[2 * phase + 1, item]
        both = pair.at[slot]
        own_one = one < CHIP
        target = jnp.where(own_one, one, two)
        side = own_one.astype(jnp.int32)
        potential(
            both, (target, side), *constants, rows, mixed, turned, stacked, result, total
        )

        @pl.when(jnp.logical_and(jnp.logical_and(own_one, two < CHIP), one != two))
        def _():
            take_away(total, two, result, both, 0)

        return carry

    lax.fori_loop(0, found, step, 0)


def visit_pairs(phase, work, buffers, constants, before):
    smem = pl.BlockSpec(memory_space=pltpu.SMEM)
    vmem = pl.BlockSpec(memory_space=pltpu.VMEM)
    anywhere = pl.BlockSpec(memory_space=pl.ANY)
    hbm = pl.BlockSpec(memory_space=pltpu.HBM)
    shape = (OWN if phase == LAST else CHIP, POINTS, POINTS * POINTS)
    extra = [] if before is None else [before]
    guess = 5
    return pl.pallas_call(
        functools.partial(visit, phase),
        out_shape=jax.ShapeDtypeStruct(shape, F32),
        in_specs=[smem, hbm] + [anywhere] * (len(buffers) - 1) + [vmem] * (2 + len(extra)),
        out_specs=vmem,
        scratch_shapes=[
            pltpu.VMEM((2, 2, POINTS, POINTS * POINTS), BF16),
            pltpu.VMEM((POINTS * HALF, 256), BF16),
            pltpu.VMEM((HALF * PITCH_A, 128), F32),
            pltpu.VMEM((POINTS * PITCH_B, 128), F32),
            pltpu.VMEM((2 * POINTS, POINTS * POINTS), BF16),
            pltpu.VMEM((POINTS, POINTS * POINTS), F32),
            pltpu.SemaphoreType.DMA((2, 2)),
        ],
        input_output_aliases={1 + len(buffers) + 2: 0} if 0 < phase < LAST else {},
        compiler_params=pltpu.CompilerParams(vmem_limit_bytes=24 << 20),
        cost_estimate=pl.CostEstimate(
            flops=guess * 3_000_000_000, bytes_accessed=guess << 20, transcendentals=0
        ),
    )(work, *buffers, *constants, *extra)


def moved(value, send):
    count = lax.axis_size("orb")
    pairs = [(source, send(source)) for source in range(count)]
    pairs = [(source, target % count) for source, target in pairs if target is not None]
    return lax.ppermute(value, "orb", pairs)


def swapped(value):
    return moved(value, lambda source: source ^ 1)


def outward(value):
    return moved(value, lambda source: source - 2 if source % 2 == 0 else source + 2)


def onward(value):
    return moved(value, lambda source: source - 1 if source % 2 == 0 else source + 1)


def exchange(orbitals, pair_list, pair_counts):
    sine, base = tables()
    row = jnp.concatenate([pair_list.reshape(-1), pair_counts])
    row = jnp.pad(row, (0, 128 - row.shape[0])).reshape(1, 128)
    rows = shared(row)
    rows, orbitals = lax.optimization_barrier((rows, orbitals))
    first = outward(orbitals)
    beside = swapped(orbitals)
    work = planned(rows)
    constants = [sine, filled_tables(base)]

    def visited(phase, buffers, total):
        return visit_pairs(phase, work, buffers, constants, total)

    third = outward(beside)
    buffers = [orbitals, beside]
    total = visited(0, buffers, None)
    first, total = lax.optimization_barrier((first, total))
    second = onward(first)
    first_beside = swapped(first)
    buffers = buffers + [first]
    total = visited(1, buffers, total)
    buffers = buffers + [first_beside]
    total = visited(2, buffers, total)
    third, total = lax.optimization_barrier((third, total))
    third_beside = swapped(third)
    buffers = buffers + [third]
    total = visited(3, buffers, total)
    buffers = buffers + [third_beside]
    total = visited(4, buffers, total)
    given = swapped(total[OWN:])
    return visited(5, buffers + [second], total) + given


def solution(mesh):
    return jax.shard_map(
        exchange,
        mesh=mesh,
        in_specs=(P("orb", None, None), P("orb", None), P("orb")),
        out_specs=P("orb", None, None),
        check_vma=False,
    )
```

```python
import functools
import math

import jax
import jax.numpy as jnp
import numpy as np
from jax import lax
from jax.experimental import pallas as pl
from jax.experimental.pallas import tpu as pltpu
from jax.sharding import PartitionSpec as P


REACH = 3
OWN = 4
SLOTS = 16
POINTS = 64
HALF = POINTS // 2
SCREENING = 0.5
LAST_BUFFER = (2, 3, 4, 5, 6, 7)
LAST = len(LAST_BUFFER) - 1
CAPS = (2, 4, 5)
CHIP = 2 * OWN
EVENS = (6, 5, 3, 0, 1, 2, 4, 6)
ODDS = (6, 4, 2, 1, 0, 3, 5, 6)
COUNTS = 2 * LAST + 2
BF16 = jnp.bfloat16
F32 = jnp.float32


def split_table(table):
    high = table.astype(np.float32).astype(BF16)
    low = (table - high.astype(np.float64)).astype(np.float32).astype(BF16)
    return high, low


def tables():
    modes = np.arange(POINTS, dtype=np.float64) + 1.0
    sines = np.sin(math.pi * modes[:, None] * modes[None, :] / (POINTS + 1))
    high, low = split_table(sines)
    left_x = np.concatenate([high, high, low], 1)
    none = np.zeros((POINTS, POINTS), BF16)

    def twice(block):
        return np.block([[block, none], [none, block]])

    right_z = np.concatenate([np.concatenate([twice(high), twice(low)], 1)] * 2, 0)
    even, odd = sines[:HALF, 0::2], sines[:HALF, 1::2]

    def thrice(block):
        upper, lower = split_table(block)
        return np.concatenate([upper, upper, lower], 1)

    left_y = np.concatenate([thrice(even), thrice(odd)], 0)
    back_y = np.concatenate([thrice(even.T), thrice(odd.T)], 0)

    def wide(block):
        return np.pad(block, ((0, 0), (0, 256 - block.shape[1])))

    sine = np.concatenate([wide(left_x), wide(left_y), wide(back_y), right_z], 0)
    base = eigenvalues()[None, :] + eigenvalues()[:, None] + SCREENING
    base = np.concatenate([base, base], 1).astype(np.float32)
    return sine, np.stack([base[:HALF], base[::-1][:HALF]])


def eigenvalues():
    modes = np.arange(POINTS, dtype=np.float64) + 1.0
    return 4.0 * np.sin(math.pi * modes / (2.0 * (POINTS + 1))) ** 2


def parts(values):
    high = values.astype(BF16)
    low = (values - high.astype(F32)).astype(BF16)
    return high, low


def dot(left, right):
    return jnp.dot(left, right, preferred_element_type=F32)


def along_first(table, values):
    high, low = parts(values)
    return dot(table, jnp.concatenate([high, low, high], 0))


def along_last(rows, table):
    both = dot(rows, table)
    return both[:, :128] + both[:, 128:]


def side_by_side(values):
    high, low = parts(values)
    return jnp.concatenate([high, low], 1)


UNROLL_A = 16
UNROLL_Z = 8
UNROLL_B = 32
UNROLL_C = 16
PITCH_A = 72
PITCH_B = 40


def chunks(count, unroll, body):
    def step(first, carry):
        for k in range(unroll):
            body(first * unroll + k)
        return carry

    if unroll == count:
        for k in range(count):
            body(k)
    else:
        lax.fori_loop(0, count // unroll, step, 0)


def aligned(start, size):
    return pl.ds(start if isinstance(start, int) else pl.multiple_of(start, 8), size)


def lanes_of(c):
    return pl.ds(c * 256 if isinstance(c, int) else pl.multiple_of(c * 256, 256), 256)


def potential(pair, target, sine, plus, minus, rows, mixed, turned, stacked, result, total):
    left_x = sine[:POINTS, : 3 * POINTS]
    left_y = sine[POINTS : 2 * POINTS, : 3 * HALF]
    back_y = sine[2 * POINTS : 3 * POINTS, : 3 * HALF]
    right_z = sine[3 * POINTS :, :]

    def forward_x(c):
        lanes = lanes_of(c)
        density = pair[0, :, lanes].astype(F32) * pair[1, :, lanes].astype(F32)
        high, low = parts(along_first(left_x, density))
        for s in range(2):
            place = aligned((2 * c + s) * POINTS, POINTS)
            rows[place, :128] = high[:, 128 * s : 128 * s + 128]
            rows[place, 128:] = low[:, 128 * s : 128 * s + 128]

    chunks(16, UNROLL_A, forward_x)

    def forward_z(c):
        out = along_last(rows[aligned(c * 256, 256), :], right_z)
        for s in range(4):
            mixed[aligned((4 * c + s) * PITCH_A, POINTS), :] = out[POINTS * s : POINTS * s + POINTS]

    chunks(8, UNROLL_Z, forward_z)

    lane = lax.broadcasted_iota(jnp.int32, (HALF, 256), 1)
    first = (lane % 128) < 64

    def middle(c):
        x = c * 2
        taken = [mixed[pl.ds(x + s, HALF, stride=PITCH_A), :] for s in range(2)]
        out = along_first(left_y, jnp.concatenate(taken, 1))
        held = jnp.where(first, out[:HALF], out[HALF:])
        other = jnp.concatenate(
            [pltpu.roll(held[:, :128], 64, 1), pltpu.roll(held[:, 128:], 64, 1)], 1
        )
        up = jnp.concatenate([plus[x], plus[x + 1]], 1)
        down = jnp.concatenate([minus[x], minus[x + 1]], 1)
        back = along_first(back_y, up * held + down * other)
        kept = jnp.where(first, back[:HALF], back[HALF:])
        for s in range(2):
            turned[aligned((x + s) * PITCH_B, HALF), :] = kept[:, 128 * s : 128 * s + 128]

    chunks(32, UNROLL_B, middle)

    def inverse_z(c):
        taken = [side_by_side(turned[pl.ds(4 * c + s, POINTS, stride=PITCH_B), :]) for s in range(4)]
        out = along_last(jnp.concatenate(taken, 0), right_z)
        high, low = parts(out)
        for s in range(4):
            lanes = pl.ds((4 * c + s) * 128 if isinstance(c, int) else pl.multiple_of((4 * c + s) * 128, 128), 128)
            stacked[:POINTS, lanes] = high[POINTS * s : POINTS * s + POINTS]
            stacked[POINTS:, lanes] = low[POINTS * s : POINTS * s + POINTS]

    chunks(8, UNROLL_Z, inverse_z)
    position, side = target

    def inverse_x(c):
        lanes = lanes_of(c)
        high, low = stacked[:POINTS, lanes], stacked[POINTS:, lanes]
        out = dot(left_x, jnp.concatenate([high, low, high], 0))
        result[:, lanes] = out
        total[position, :, lanes] -= out * pair[side, :, lanes].astype(F32)

    chunks(16, UNROLL_C, inverse_x)


def take_away(total, position, result, pair, side):
    def step(c, carry):
        lanes = pl.ds(pl.multiple_of(c * 256, 256), 256)
        total[position, :, lanes] -= result[:, lanes] * pair[side, :, lanes].astype(F32)
        return carry

    lax.fori_loop(0, 16, step, 0, unroll=4)


def fill_tables(base, out):
    for x, value in enumerate(eigenvalues()):
        scale = (2.0 / (POINTS + 1)) ** 3
        near = scale / (base[0] + np.float32(value))
        far = scale / (base[1] + np.float32(value))
        out[0, x] = near + far
        out[1, x] = near - far


def filled_tables(base):
    vmem = pl.BlockSpec(memory_space=pltpu.VMEM)
    return pl.pallas_call(
        fill_tables,
        out_shape=jax.ShapeDtypeStruct((2, POINTS, HALF, 128), F32),
        in_specs=[vmem],
        out_specs=vmem,
        name="fill_tables",
    )(base)


def share(row, out, send_sems, recv_sems, own_sem):
    me = lax.axis_index("orb")
    count = lax.axis_size("orb")
    odd = me % 2

    def device(at):
        return (lax.rem(at + count, count),)

    def signal(at):
        pl.semaphore_signal(
            barrier, inc=1, device_id=device(at), device_id_type=pl.DeviceIdType.MESH
        )

    def remote(source, target, send, receive, at):
        return pltpu.make_async_remote_copy(
            src_ref=source,
            dst_ref=target,
            send_sem=send_sems.at[send],
            recv_sem=recv_sems.at[receive],
            device_id=device(at),
            device_id_type=pl.DeviceIdType.MESH,
        )

    barrier = pltpu.get_barrier_semaphore()
    partner = me + 1 - 2 * odd
    signal(partner)
    signal(me - 2 - odd)
    signal(me - 4 - odd)

    @pl.when(odd == 0)
    def _():
        pl.semaphore_wait(barrier, 5)

    @pl.when(odd == 1)
    def _():
        pl.semaphore_wait(barrier, 1)

    local = pltpu.make_async_copy(row, out.at[0], own_sem)
    first = remote(row, out.at[1], 0, 0, partner)
    local.start()
    first.start()
    local.wait()
    first.wait()
    two = out.at[pl.ds(0, 2)], out.at[pl.ds(2, 2)]
    one = out.at[1], out.at[4]
    sends = [
        remote(*pair, k + 1, 1 + k // 2, me + 2 + k)
        for k, pair in enumerate((two, two, one, one))
    ]

    @pl.when(odd == 0)
    def _():
        for send in sends:
            send.start()

    sends[0].wait_recv()
    sends[2].wait_recv()

    @pl.when(odd == 0)
    def _():
        for send in sends:
            send.wait_send()


def shared(row):
    vmem = pl.BlockSpec(memory_space=pltpu.VMEM)
    return pl.pallas_call(
        share,
        out_shape=jax.ShapeDtypeStruct((5, 1, 128), jnp.int32),
        in_specs=[vmem],
        out_specs=vmem,
        scratch_shapes=[
            pltpu.SemaphoreType.DMA((5,)),
            pltpu.SemaphoreType.DMA((3,)),
            pltpu.SemaphoreType.DMA,
        ],
        compiler_params=pltpu.CompilerParams(collective_id=0, has_side_effects=True),
        name="share",
    )(row)


def plan(rows, work, buffer_of):
    odd = lax.axis_index("orb") % 2
    is_odd = odd == 1
    for k in range(8):
        buffer_of[k] = jnp.where(is_odd, ODDS[k], EVENS[k])
    for phase in range(LAST + 1):
        work[COUNTS, phase] = 0

    def put(one_at, one, two_at, two, take):
        phase = jnp.maximum(jnp.maximum(one_at, two_at) - 1, 0)
        for early in range(len(CAPS)):
            full = jnp.logical_and(phase == early, work[COUNTS, early] >= CAPS[early])
            phase = jnp.where(full, early + 1, phase)
        count = work[COUNTS, phase]
        work[2 * phase, count] = one_at * OWN + one
        work[2 * phase + 1, count] = two_at * OWN + two
        work[COUNTS, phase] = count + take.astype(jnp.int32)

    def reach_of(w):
        return lax.shift_right_logical(w, 2)

    def visit_far(slot, found):
        w = rows[4, 0, 2 * slot + 1]
        reaches = reach_of(w) == REACH
        index = lax.bitwise_and(w, OWN - 1)
        mine = jnp.logical_and(reaches, jnp.logical_not(is_odd))
        put(buffer_of[0], rows[4, 0, 2 * slot], buffer_of[REACH], index, mine)
        return found + reaches.astype(jnp.int32)

    lead = lax.fori_loop(0, rows[4, 0, 2 * SLOTS], visit_far, jnp.int32(0))
    upper = 1 - odd

    def count_far(slot, lead):
        return lead - (reach_of(rows[upper, 0, 2 * slot + 1]) == REACH).astype(jnp.int32)

    lead = lax.fori_loop(0, rows[upper, 0, 2 * SLOTS], count_far, lead)
    for base, which in enumerate((2, 3, odd, upper), 1):

        def visit_row(slot, lead, base=base, which=which):
            a = rows[which, 0, 2 * slot]
            w = rows[which, 0, 2 * slot + 1]
            place = base + reach_of(w)
            to_odd = (lead > 0).astype(jnp.int32)
            if base >= REACH:
                shared = place < REACH + OWN
                mine = jnp.where(shared, to_odd == odd, is_odd)
            else:
                shared = jnp.logical_or(place == REACH, place == REACH + 1)
                mine = jnp.logical_and(shared, to_odd == odd)
            put(buffer_of[base], a, buffer_of[place], lax.bitwise_and(w, OWN - 1), mine)
            return jnp.where(shared, lead + 1 - 2 * to_odd, lead)

        lead = lax.fori_loop(0, rows[which, 0, 2 * SLOTS], visit_row, lead)


def planned(rows):
    smem = pl.BlockSpec(memory_space=pltpu.SMEM)
    return pl.pallas_call(
        plan,
        out_shape=jax.ShapeDtypeStruct((COUNTS + 1, 5 * SLOTS + 1), jnp.int32),
        in_specs=[smem],
        out_specs=smem,
        scratch_shapes=[pltpu.SMEM((8,), jnp.int32)],
        name="plan",
    )(rows)


def visit(phase, *refs):
    work = refs[0]
    held = LAST_BUFFER[phase]
    buffers = refs[1 : 1 + held]
    rest = list(refs[1 + held :])
    constants = [rest[0], rest[1].at[0], rest[1].at[1]]
    rest = rest[2:]
    before = rest.pop(0) if phase > 0 else None
    given = rest.pop(0)
    pair, rows, mixed, turned, stacked, result, sems = rest[:7]
    total = given
    found = work[COUNTS, phase]

    def fetch(item, slot):
        for side in range(2):
            code = work[2 * phase + side, item]
            at = code // OWN
            index = code % OWN
            for b in range(held):
                @pl.when(at == b)
                def _():
                    pltpu.make_async_copy(
                        buffers[b].at[index], pair.at[slot, side], sems.at[slot, side]
                    ).start()

    @pl.when(found > 0)
    def _():
        fetch(0, 0)

    if phase == 0:
        total[...] = jnp.zeros_like(total)
    if phase == LAST:
        total[...] = before[:OWN]

    def step(item, carry):
        slot = item % 2
        for side in range(2):
            pltpu.make_async_copy(
                buffers[0].at[0], pair.at[slot, side], sems.at[slot, side]
            ).wait()

        @pl.when(item + 1 < found)
        def _():
            fetch(item + 1, 1 - slot)

        one = work[2 * phase, item]
        two = work[2 * phase + 1, item]
        both = pair.at[slot]
        own_one = one < CHIP
        target = jnp.where(own_one, one, two)
        side = own_one.astype(jnp.int32)
        potential(
            both, (target, side), *constants, rows, mixed, turned, stacked, result, total
        )

        @pl.when(jnp.logical_and(jnp.logical_and(own_one, two < CHIP), one != two))
        def _():
            take_away(total, two, result, both, 0)

        return carry

    lax.fori_loop(0, found, step, 0)


def visit_pairs(phase, work, buffers, constants, before):
    smem = pl.BlockSpec(memory_space=pltpu.SMEM)
    vmem = pl.BlockSpec(memory_space=pltpu.VMEM)
    anywhere = pl.BlockSpec(memory_space=pl.ANY)
    hbm = pl.BlockSpec(memory_space=pltpu.HBM)
    shape = (OWN if phase == LAST else CHIP, POINTS, POINTS * POINTS)
    extra = [] if before is None else [before]
    guess = 5
    return pl.pallas_call(
        functools.partial(visit, phase),
        out_shape=jax.ShapeDtypeStruct(shape, F32),
        in_specs=[smem, hbm] + [anywhere] * (len(buffers) - 1) + [vmem] * (2 + len(extra)),
        out_specs=vmem,
        scratch_shapes=[
            pltpu.VMEM((2, 2, POINTS, POINTS * POINTS), BF16),
            pltpu.VMEM((POINTS * HALF, 256), BF16),
            pltpu.VMEM((HALF * PITCH_A, 128), F32),
            pltpu.VMEM((POINTS * PITCH_B, 128), F32),
            pltpu.VMEM((2 * POINTS, POINTS * POINTS), BF16),
            pltpu.VMEM((POINTS, POINTS * POINTS), F32),
            pltpu.SemaphoreType.DMA((2, 2)),
        ],
        input_output_aliases={1 + len(buffers) + 2: 0} if 0 < phase < LAST else {},
        compiler_params=pltpu.CompilerParams(vmem_limit_bytes=24 << 20),
        cost_estimate=pl.CostEstimate(
            flops=guess * 3_000_000_000, bytes_accessed=guess << 20, transcendentals=0
        ),
    )(work, *buffers, *constants, *extra)


def moved(value, send):
    count = lax.axis_size("orb")
    pairs = [(source, send(source)) for source in range(count)]
    pairs = [(source, target % count) for source, target in pairs if target is not None]
    return lax.ppermute(value, "orb", pairs)


def swapped(value):
    return moved(value, lambda source: source ^ 1)


def outward(value):
    return moved(value, lambda source: source - 2 if source % 2 == 0 else source + 2)


def onward(value):
    return moved(value, lambda source: source - 1 if source % 2 == 0 else source + 1)


def exchange(orbitals, pair_list, pair_counts):
    sine, base = tables()
    row = jnp.concatenate([pair_list.reshape(-1), pair_counts])
    row = jnp.pad(row, (0, 128 - row.shape[0])).reshape(1, 128)
    rows = shared(row)
    first = outward(orbitals)
    rows, orbitals = lax.optimization_barrier((rows, orbitals))
    beside = swapped(orbitals)
    work = planned(rows)
    constants = [sine, filled_tables(base)]

    def visited(phase, buffers, total):
        return visit_pairs(phase, work, buffers, constants, total)

    third = outward(beside)
    buffers = [orbitals, beside]
    total = visited(0, buffers, None)
    first, total = lax.optimization_barrier((first, total))
    second = onward(first)
    first_beside = swapped(first)
    buffers = buffers + [first]
    total = visited(1, buffers, total)
    buffers = buffers + [first_beside]
    total = visited(2, buffers, total)
    third, total = lax.optimization_barrier((third, total))
    third_beside = swapped(third)
    buffers = buffers + [third]
    total = visited(3, buffers, total)
    buffers = buffers + [third_beside]
    total = visited(4, buffers, total)
    given = swapped(total[OWN:])
    return visited(5, buffers + [second], total) + given


def solution(mesh):
    return jax.shard_map(
        exchange,
        mesh=mesh,
        in_specs=(P("orb", None, None), P("orb", None), P("orb")),
        out_specs=P("orb", None, None),
        check_vma=False,
    )
```

```python
import functools
import math

import jax
import jax.numpy as jnp
import numpy as np
from jax import lax
from jax.experimental import pallas as pl
from jax.experimental.pallas import tpu as pltpu
from jax.sharding import PartitionSpec as P


REACH = 3
OWN = 4
SLOTS = 16
POINTS = 64
HALF = POINTS // 2
SCREENING = 0.5
LAST_BUFFER = (2, 3, 4, 5, 6, 7)
LAST = len(LAST_BUFFER) - 1
CAPS = (5, 4, 5)
CHIP = 2 * OWN
EVENS = (6, 5, 3, 0, 1, 2, 4, 6)
ODDS = (6, 4, 2, 1, 0, 3, 5, 6)
COUNTS = 2 * LAST + 2
BF16 = jnp.bfloat16
F32 = jnp.float32


def split_table(table):
    high = table.astype(np.float32).astype(BF16)
    low = (table - high.astype(np.float64)).astype(np.float32).astype(BF16)
    return high, low


def tables():
    modes = np.arange(POINTS, dtype=np.float64) + 1.0
    sines = np.sin(math.pi * modes[:, None] * modes[None, :] / (POINTS + 1))
    high, low = split_table(sines)
    left_x = np.concatenate([high, high, low], 1)
    none = np.zeros((POINTS, POINTS), BF16)

    def twice(block):
        return np.block([[block, none], [none, block]])

    right_z = np.concatenate([np.concatenate([twice(high), twice(low)], 1)] * 2, 0)
    even, odd = sines[:HALF, 0::2], sines[:HALF, 1::2]

    def thrice(block):
        upper, lower = split_table(block)
        return np.concatenate([upper, upper, lower], 1)

    left_y = np.concatenate([thrice(even), thrice(odd)], 0)
    back_y = np.concatenate([thrice(even.T), thrice(odd.T)], 0)

    def wide(block):
        return np.pad(block, ((0, 0), (0, 256 - block.shape[1])))

    sine = np.concatenate([wide(left_x), wide(left_y), wide(back_y), right_z], 0)
    base = eigenvalues()[None, :] + eigenvalues()[:, None] + SCREENING
    base = np.concatenate([base, base], 1).astype(np.float32)
    return sine, np.stack([base[:HALF], base[::-1][:HALF]])


def eigenvalues():
    modes = np.arange(POINTS, dtype=np.float64) + 1.0
    return 4.0 * np.sin(math.pi * modes / (2.0 * (POINTS + 1))) ** 2


def parts(values):
    high = values.astype(BF16)
    low = (values - high.astype(F32)).astype(BF16)
    return high, low


def dot(left, right):
    return jnp.dot(left, right, preferred_element_type=F32)


def along_first(table, values):
    high, low = parts(values)
    return dot(table, jnp.concatenate([high, low, high], 0))


def along_last(rows, table):
    both = dot(rows, table)
    return both[:, :128] + both[:, 128:]


def side_by_side(values):
    high, low = parts(values)
    return jnp.concatenate([high, low], 1)


UNROLL_A = 16
UNROLL_Z = 8
UNROLL_B = 32
UNROLL_C = 16
PITCH_A = 72
PITCH_B = 40


def chunks(count, unroll, body):
    def step(first, carry):
        for k in range(unroll):
            body(first * unroll + k)
        return carry

    if unroll == count:
        for k in range(count):
            body(k)
    else:
        lax.fori_loop(0, count // unroll, step, 0)


def aligned(start, size):
    return pl.ds(start if isinstance(start, int) else pl.multiple_of(start, 8), size)


def lanes_of(c):
    return pl.ds(c * 256 if isinstance(c, int) else pl.multiple_of(c * 256, 256), 256)


def potential(pair, target, sine, plus, minus, rows, mixed, turned, stacked, result, total):
    left_x = sine[:POINTS, : 3 * POINTS]
    left_y = sine[POINTS : 2 * POINTS, : 3 * HALF]
    back_y = sine[2 * POINTS : 3 * POINTS, : 3 * HALF]
    right_z = sine[3 * POINTS :, :]

    def forward_x(c):
        lanes = lanes_of(c)
        density = pair[0, :, lanes].astype(F32) * pair[1, :, lanes].astype(F32)
        high, low = parts(along_first(left_x, density))
        for s in range(2):
            place = aligned((2 * c + s) * POINTS, POINTS)
            rows[place, :128] = high[:, 128 * s : 128 * s + 128]
            rows[place, 128:] = low[:, 128 * s : 128 * s + 128]

    chunks(16, UNROLL_A, forward_x)

    def forward_z(c):
        out = along_last(rows[aligned(c * 256, 256), :], right_z)
        for s in range(4):
            mixed[aligned((4 * c + s) * PITCH_A, POINTS), :] = out[POINTS * s : POINTS * s + POINTS]

    chunks(8, UNROLL_Z, forward_z)

    lane = lax.broadcasted_iota(jnp.int32, (HALF, 256), 1)
    first = (lane % 128) < 64

    def middle(c):
        x = c * 2
        taken = [mixed[pl.ds(x + s, HALF, stride=PITCH_A), :] for s in range(2)]
        out = along_first(left_y, jnp.concatenate(taken, 1))
        held = jnp.where(first, out[:HALF], out[HALF:])
        other = jnp.concatenate(
            [pltpu.roll(held[:, :128], 64, 1), pltpu.roll(held[:, 128:], 64, 1)], 1
        )
        up = jnp.concatenate([plus[x], plus[x + 1]], 1)
        down = jnp.concatenate([minus[x], minus[x + 1]], 1)
        back = along_first(back_y, up * held + down * other)
        kept = jnp.where(first, back[:HALF], back[HALF:])
        for s in range(2):
            turned[aligned((x + s) * PITCH_B, HALF), :] = kept[:, 128 * s : 128 * s + 128]

    chunks(32, UNROLL_B, middle)

    def inverse_z(c):
        taken = [side_by_side(turned[pl.ds(4 * c + s, POINTS, stride=PITCH_B), :]) for s in range(4)]
        out = along_last(jnp.concatenate(taken, 0), right_z)
        high, low = parts(out)
        for s in range(4):
            lanes = pl.ds((4 * c + s) * 128 if isinstance(c, int) else pl.multiple_of((4 * c + s) * 128, 128), 128)
            stacked[:POINTS, lanes] = high[POINTS * s : POINTS * s + POINTS]
            stacked[POINTS:, lanes] = low[POINTS * s : POINTS * s + POINTS]

    chunks(8, UNROLL_Z, inverse_z)
    position, side = target

    def inverse_x(c):
        lanes = lanes_of(c)
        high, low = stacked[:POINTS, lanes], stacked[POINTS:, lanes]
        out = dot(left_x, jnp.concatenate([high, low, high], 0))
        result[:, lanes] = out
        total[position, :, lanes] -= out * pair[side, :, lanes].astype(F32)

    chunks(16, UNROLL_C, inverse_x)


def take_away(total, position, result, pair, side):
    def step(c, carry):
        lanes = pl.ds(pl.multiple_of(c * 256, 256), 256)
        total[position, :, lanes] -= result[:, lanes] * pair[side, :, lanes].astype(F32)
        return carry

    lax.fori_loop(0, 16, step, 0, unroll=4)


def fill_tables(base, out):
    for x, value in enumerate(eigenvalues()):
        scale = (2.0 / (POINTS + 1)) ** 3
        near = scale / (base[0] + np.float32(value))
        far = scale / (base[1] + np.float32(value))
        out[0, x] = near + far
        out[1, x] = near - far


def filled_tables(base):
    vmem = pl.BlockSpec(memory_space=pltpu.VMEM)
    return pl.pallas_call(
        fill_tables,
        out_shape=jax.ShapeDtypeStruct((2, POINTS, HALF, 128), F32),
        in_specs=[vmem],
        out_specs=vmem,
        name="fill_tables",
    )(base)


def share(row, out, send_sems, recv_sems, own_sem):
    me = lax.axis_index("orb")
    count = lax.axis_size("orb")
    odd = me % 2

    def device(at):
        return (lax.rem(at + count, count),)

    def signal(at):
        pl.semaphore_signal(
            barrier, inc=1, device_id=device(at), device_id_type=pl.DeviceIdType.MESH
        )

    def remote(source, target, send, receive, at):
        return pltpu.make_async_remote_copy(
            src_ref=source,
            dst_ref=target,
            send_sem=send_sems.at[send],
            recv_sem=recv_sems.at[receive],
            device_id=device(at),
            device_id_type=pl.DeviceIdType.MESH,
        )

    barrier = pltpu.get_barrier_semaphore()
    partner = me + 1 - 2 * odd
    for source in (partner, me - 2, me - 1 - 2 * odd, me - 3 - odd):
        signal(source)

    @pl.when(odd == 0)
    def _():
        pl.semaphore_wait(barrier, 3)

    @pl.when(odd == 1)
    def _():
        pl.semaphore_wait(barrier, 5)

    local = pltpu.make_async_copy(row, out.at[0], own_sem)
    local.start()
    copies = [
        remote(row, out.at[1], 0, 0, partner),
        remote(row, out.at[2], 1, 1, me + 2),
        remote(row, out.at[3], 2, 2, me + 3 - 2 * odd),
    ]
    far = [remote(row, out.at[4], 3 + k, 3, me + 3 + k) for k in range(2)]
    for copy in copies:
        copy.start()

    @pl.when(odd == 1)
    def _():
        for copy in far:
            copy.start()

    local.wait()
    for copy in copies:
        copy.wait()
    far[0].wait_recv()

    @pl.when(odd == 1)
    def _():
        for copy in far:
            copy.wait_send()


def shared(row):
    vmem = pl.BlockSpec(memory_space=pltpu.VMEM)
    return pl.pallas_call(
        share,
        out_shape=jax.ShapeDtypeStruct((5, 1, 128), jnp.int32),
        in_specs=[vmem],
        out_specs=vmem,
        scratch_shapes=[
            pltpu.SemaphoreType.DMA((5,)),
            pltpu.SemaphoreType.DMA((4,)),
            pltpu.SemaphoreType.DMA,
        ],
        compiler_params=pltpu.CompilerParams(collective_id=0, has_side_effects=True),
        name="share",
    )(row)


def plan(rows, work, buffer_of):
    odd = lax.axis_index("orb") % 2
    is_odd = odd == 1
    for k in range(8):
        buffer_of[k] = jnp.where(is_odd, ODDS[k], EVENS[k])
    for phase in range(LAST + 1):
        work[COUNTS, phase] = 0

    def put(one_at, one, two_at, two, take):
        phase = jnp.maximum(jnp.maximum(one_at, two_at) - 1, 0)
        for early in range(len(CAPS)):
            full = jnp.logical_and(phase == early, work[COUNTS, early] >= CAPS[early])
            phase = jnp.where(full, early + 1, phase)
        count = work[COUNTS, phase]
        work[2 * phase, count] = one_at * OWN + one
        work[2 * phase + 1, count] = two_at * OWN + two
        work[COUNTS, phase] = count + take.astype(jnp.int32)

    def reach_of(w):
        return lax.shift_right_logical(w, 2)

    def visit_far(slot, found):
        w = rows[4, 0, 2 * slot + 1]
        reaches = reach_of(w) == REACH
        index = lax.bitwise_and(w, OWN - 1)
        mine = jnp.logical_and(reaches, jnp.logical_not(is_odd))
        put(buffer_of[0], rows[4, 0, 2 * slot], buffer_of[REACH], index, mine)
        return found + reaches.astype(jnp.int32)

    lead = lax.fori_loop(0, rows[4, 0, 2 * SLOTS], visit_far, jnp.int32(0))
    upper = 1 - odd

    def count_far(slot, lead):
        return lead - (reach_of(rows[upper, 0, 2 * slot + 1]) == REACH).astype(jnp.int32)

    lead = lax.fori_loop(0, rows[upper, 0, 2 * SLOTS], count_far, lead)
    for base, which in enumerate((2 + odd, 3 - odd, odd, upper), 1):

        def visit_row(slot, lead, base=base, which=which):
            a = rows[which, 0, 2 * slot]
            w = rows[which, 0, 2 * slot + 1]
            place = base + reach_of(w)
            to_odd = (lead > 0).astype(jnp.int32)
            if base >= REACH:
                shared = place < REACH + OWN
                mine = jnp.where(shared, to_odd == odd, is_odd)
            else:
                shared = jnp.logical_or(place == REACH, place == REACH + 1)
                mine = jnp.logical_and(shared, to_odd == odd)
            put(buffer_of[base], a, buffer_of[place], lax.bitwise_and(w, OWN - 1), mine)
            return jnp.where(shared, lead + 1 - 2 * to_odd, lead)

        lead = lax.fori_loop(0, rows[which, 0, 2 * SLOTS], visit_row, lead)


def planned(rows):
    smem = pl.BlockSpec(memory_space=pltpu.SMEM)
    return pl.pallas_call(
        plan,
        out_shape=jax.ShapeDtypeStruct((COUNTS + 1, 5 * SLOTS + 1), jnp.int32),
        in_specs=[smem],
        out_specs=smem,
        scratch_shapes=[pltpu.SMEM((8,), jnp.int32)],
        name="plan",
    )(rows)


def visit(phase, *refs):
    work = refs[0]
    held = LAST_BUFFER[phase]
    buffers = refs[1 : 1 + held]
    rest = list(refs[1 + held :])
    constants = [rest[0], rest[1].at[0], rest[1].at[1]]
    rest = rest[2:]
    before = rest.pop(0) if phase > 0 else None
    given = rest.pop(0)
    pair, rows, mixed, turned, stacked, result, sems = rest[:7]
    total = given
    found = work[COUNTS, phase]

    def fetch(item, slot):
        for side in range(2):
            code = work[2 * phase + side, item]
            at = code // OWN
            index = code % OWN
            for b in range(held):
                @pl.when(at == b)
                def _():
                    pltpu.make_async_copy(
                        buffers[b].at[index], pair.at[slot, side], sems.at[slot, side]
                    ).start()

    @pl.when(found > 0)
    def _():
        fetch(0, 0)

    if phase == 0:
        total[...] = jnp.zeros_like(total)
    if phase == LAST:
        total[...] = before[:OWN]

    def step(item, carry):
        slot = item % 2
        for side in range(2):
            pltpu.make_async_copy(
                buffers[0].at[0], pair.at[slot, side], sems.at[slot, side]
            ).wait()

        @pl.when(item + 1 < found)
        def _():
            fetch(item + 1, 1 - slot)

        one = work[2 * phase, item]
        two = work[2 * phase + 1, item]
        both = pair.at[slot]
        own_one = one < CHIP
        target = jnp.where(own_one, one, two)
        side = own_one.astype(jnp.int32)
        potential(
            both, (target, side), *constants, rows, mixed, turned, stacked, result, total
        )

        @pl.when(jnp.logical_and(jnp.logical_and(own_one, two < CHIP), one != two))
        def _():
            take_away(total, two, result, both, 0)

        return carry

    lax.fori_loop(0, found, step, 0)


def visit_pairs(phase, work, buffers, constants, before):
    smem = pl.BlockSpec(memory_space=pltpu.SMEM)
    vmem = pl.BlockSpec(memory_space=pltpu.VMEM)
    anywhere = pl.BlockSpec(memory_space=pl.ANY)
    hbm = pl.BlockSpec(memory_space=pltpu.HBM)
    shape = (OWN if phase == LAST else CHIP, POINTS, POINTS * POINTS)
    extra = [] if before is None else [before]
    guess = 5
    return pl.pallas_call(
        functools.partial(visit, phase),
        out_shape=jax.ShapeDtypeStruct(shape, F32),
        in_specs=[smem, hbm] + [anywhere] * (len(buffers) - 1) + [vmem] * (2 + len(extra)),
        out_specs=vmem,
        scratch_shapes=[
            pltpu.VMEM((2, 2, POINTS, POINTS * POINTS), BF16),
            pltpu.VMEM((POINTS * HALF, 256), BF16),
            pltpu.VMEM((HALF * PITCH_A, 128), F32),
            pltpu.VMEM((POINTS * PITCH_B, 128), F32),
            pltpu.VMEM((2 * POINTS, POINTS * POINTS), BF16),
            pltpu.VMEM((POINTS, POINTS * POINTS), F32),
            pltpu.SemaphoreType.DMA((2, 2)),
        ],
        input_output_aliases={1 + len(buffers) + 2: 0} if 0 < phase < LAST else {},
        compiler_params=pltpu.CompilerParams(vmem_limit_bytes=24 << 20),
        cost_estimate=pl.CostEstimate(
            flops=guess * 3_000_000_000, bytes_accessed=guess << 20, transcendentals=0
        ),
    )(work, *buffers, *constants, *extra)


def moved(value, send):
    count = lax.axis_size("orb")
    pairs = [(source, send(source)) for source in range(count)]
    pairs = [(source, target % count) for source, target in pairs if target is not None]
    return lax.ppermute(value, "orb", pairs)


def swapped(value):
    return moved(value, lambda source: source ^ 1)


def outward(value):
    return moved(value, lambda source: source - 2 if source % 2 == 0 else source + 2)


def onward(value):
    return moved(value, lambda source: source - 1 if source % 2 == 0 else source + 1)


def exchange(orbitals, pair_list, pair_counts):
    sine, base = tables()
    row = jnp.concatenate([pair_list.reshape(-1), pair_counts])
    row = jnp.pad(row, (0, 128 - row.shape[0])).reshape(1, 128)
    rows = shared(row)
    rows, orbitals = lax.optimization_barrier((rows, orbitals))
    first = outward(orbitals)
    beside = swapped(orbitals)
    work = planned(rows)
    constants = [sine, filled_tables(base)]

    def visited(phase, buffers, total):
        return visit_pairs(phase, work, buffers, constants, total)

    third = outward(beside)
    buffers = [orbitals, beside]
    total = visited(0, buffers, None)
    first, total = lax.optimization_barrier((first, total))
    second = onward(first)
    first_beside = swapped(first)
    buffers = buffers + [first]
    total = visited(1, buffers, total)
    buffers = buffers + [first_beside]
    total = visited(2, buffers, total)
    third, total = lax.optimization_barrier((third, total))
    third_beside = swapped(third)
    buffers = buffers + [third]
    total = visited(3, buffers, total)
    buffers = buffers + [third_beside]
    total = visited(4, buffers, total)
    given = swapped(total[OWN:])
    return visited(5, buffers + [second], total) + given


def solution(mesh):
    return jax.shard_map(
        exchange,
        mesh=mesh,
        in_specs=(P("orb", None, None), P("orb", None), P("orb")),
        out_specs=P("orb", None, None),
        check_vma=False,
    )
```

```python
import functools
import math

import jax
import jax.numpy as jnp
import numpy as np
from jax import lax
from jax.experimental import pallas as pl
from jax.experimental.pallas import tpu as pltpu
from jax.sharding import PartitionSpec as P


REACH = 3
OWN = 4
SLOTS = 16
POINTS = 64
HALF = POINTS // 2
SCREENING = 0.5
LAST_BUFFER = (2, 3, 4, 5, 6, 7)
LAST = len(LAST_BUFFER) - 1
CAPS = (5, 5, 4)
COUNTS = 2 * LAST + 2
BF16 = jnp.bfloat16
F32 = jnp.float32


def split_table(table):
    high = table.astype(np.float32).astype(BF16)
    low = (table - high.astype(np.float64)).astype(np.float32).astype(BF16)
    return high, low


def tables():
    modes = np.arange(POINTS, dtype=np.float64) + 1.0
    sines = np.sin(math.pi * modes[:, None] * modes[None, :] / (POINTS + 1))
    high, low = split_table(sines)
    left_x = np.concatenate([high, high, low], 1)
    none = np.zeros((POINTS, POINTS), BF16)

    def twice(block):
        return np.block([[block, none], [none, block]])

    right_z = np.concatenate([np.concatenate([twice(high), twice(low)], 1)] * 2, 0)
    even, odd = sines[:HALF, 0::2], sines[:HALF, 1::2]

    def thrice(block):
        upper, lower = split_table(block)
        return np.concatenate([upper, upper, lower], 1)

    left_y = np.concatenate([thrice(even), thrice(odd)], 0)
    back_y = np.concatenate([thrice(even.T), thrice(odd.T)], 0)

    def wide(block):
        return np.pad(block, ((0, 0), (0, 256 - block.shape[1])))

    sine = np.concatenate([wide(left_x), wide(left_y), wide(back_y), right_z], 0)
    base = eigenvalues()[None, :] + eigenvalues()[:, None] + SCREENING
    base = np.concatenate([base, base], 1).astype(np.float32)
    return sine, np.stack([base[:HALF], base[::-1][:HALF]])


def eigenvalues():
    modes = np.arange(POINTS, dtype=np.float64) + 1.0
    return 4.0 * np.sin(math.pi * modes / (2.0 * (POINTS + 1))) ** 2


def parts(values):
    high = values.astype(BF16)
    low = (values - high.astype(F32)).astype(BF16)
    return high, low


def dot(left, right):
    return jnp.dot(left, right, preferred_element_type=F32)


def along_first(table, values):
    high, low = parts(values)
    return dot(table, jnp.concatenate([high, low, high], 0))


def along_last(rows, table):
    both = dot(rows, table)
    return both[:, :128] + both[:, 128:]


def side_by_side(values):
    high, low = parts(values)
    return jnp.concatenate([high, low], 1)


UNROLL_A = 16
UNROLL_Z = 8
UNROLL_B = 32
UNROLL_C = 16
PITCH_A = 72
PITCH_B = 40


def chunks(count, unroll, body):
    def step(first, carry):
        for k in range(unroll):
            body(first * unroll + k)
        return carry

    if unroll == count:
        for k in range(count):
            body(k)
    else:
        lax.fori_loop(0, count // unroll, step, 0)


def aligned(start, size):
    return pl.ds(start if isinstance(start, int) else pl.multiple_of(start, 8), size)


def lanes_of(c):
    return pl.ds(c * 256 if isinstance(c, int) else pl.multiple_of(c * 256, 256), 256)


def potential(pair, target, sine, plus, minus, rows, mixed, turned, stacked, result, total):
    left_x = sine[:POINTS, : 3 * POINTS]
    left_y = sine[POINTS : 2 * POINTS, : 3 * HALF]
    back_y = sine[2 * POINTS : 3 * POINTS, : 3 * HALF]
    right_z = sine[3 * POINTS :, :]

    def forward_x(c):
        lanes = lanes_of(c)
        density = pair[0, :, lanes].astype(F32) * pair[1, :, lanes].astype(F32)
        high, low = parts(along_first(left_x, density))
        for s in range(2):
            place = aligned((2 * c + s) * POINTS, POINTS)
            rows[place, :128] = high[:, 128 * s : 128 * s + 128]
            rows[place, 128:] = low[:, 128 * s : 128 * s + 128]

    chunks(16, UNROLL_A, forward_x)

    def forward_z(c):
        out = along_last(rows[aligned(c * 256, 256), :], right_z)
        for s in range(4):
            mixed[aligned((4 * c + s) * PITCH_A, POINTS), :] = out[POINTS * s : POINTS * s + POINTS]

    chunks(8, UNROLL_Z, forward_z)

    lane = lax.broadcasted_iota(jnp.int32, (HALF, 256), 1)
    first = (lane % 128) < 64

    def middle(c):
        x = c * 2
        taken = [mixed[pl.ds(x + s, HALF, stride=PITCH_A), :] for s in range(2)]
        out = along_first(left_y, jnp.concatenate(taken, 1))
        held = jnp.where(first, out[:HALF], out[HALF:])
        other = jnp.concatenate(
            [pltpu.roll(held[:, :128], 64, 1), pltpu.roll(held[:, 128:], 64, 1)], 1
        )
        up = jnp.concatenate([plus[x], plus[x + 1]], 1)
        down = jnp.concatenate([minus[x], minus[x + 1]], 1)
        back = along_first(back_y, up * held + down * other)
        kept = jnp.where(first, back[:HALF], back[HALF:])
        for s in range(2):
            turned[aligned((x + s) * PITCH_B, HALF), :] = kept[:, 128 * s : 128 * s + 128]

    chunks(32, UNROLL_B, middle)

    def inverse_z(c):
        taken = [side_by_side(turned[pl.ds(4 * c + s, POINTS, stride=PITCH_B), :]) for s in range(4)]
        out = along_last(jnp.concatenate(taken, 0), right_z)
        high, low = parts(out)
        for s in range(4):
            lanes = pl.ds((4 * c + s) * 128 if isinstance(c, int) else pl.multiple_of((4 * c + s) * 128, 128), 128)
            stacked[:POINTS, lanes] = high[POINTS * s : POINTS * s + POINTS]
            stacked[POINTS:, lanes] = low[POINTS * s : POINTS * s + POINTS]

    chunks(8, UNROLL_Z, inverse_z)
    position, side = target

    def inverse_x(c):
        lanes = lanes_of(c)
        high, low = stacked[:POINTS, lanes], stacked[POINTS:, lanes]
        out = dot(left_x, jnp.concatenate([high, low, high], 0))
        result[:, lanes] = out
        total[position, :, lanes] -= out * pair[side, :, lanes].astype(F32)

    chunks(16, UNROLL_C, inverse_x)


def take_away(total, position, result, pair, side):
    def step(c, carry):
        lanes = pl.ds(pl.multiple_of(c * 256, 256), 256)
        total[position, :, lanes] -= result[:, lanes] * pair[side, :, lanes].astype(F32)
        return carry

    lax.fori_loop(0, 16, step, 0, unroll=4)


def fill_tables(base, out):
    for x, value in enumerate(eigenvalues()):
        scale = (2.0 / (POINTS + 1)) ** 3
        near = scale / (base[0] + np.float32(value))
        far = scale / (base[1] + np.float32(value))
        out[0, x] = near + far
        out[1, x] = near - far


def filled_tables(base):
    vmem = pl.BlockSpec(memory_space=pltpu.VMEM)
    return pl.pallas_call(
        fill_tables,
        out_shape=jax.ShapeDtypeStruct((2, POINTS, HALF, 128), F32),
        in_specs=[vmem],
        out_specs=vmem,
        name="fill_tables",
    )(base)


def plan(row_0, row_1, row_2, row_3, work):
    odd = lax.axis_index("orb") % 2

    def buffer_of(place):
        evens = (6, 5, 3, 0, 1, 2, 4)
        odds = (4, 2, 1, 0, 3, 5, 6)
        at = jnp.int32(0)
        for k in range(2 * REACH + 1):
            at = jnp.where(place == k, jnp.where(odd == 1, odds[k], evens[k]), at)
        return at

    for phase in range(LAST + 1):
        work[COUNTS, phase] = 0
    for back, rows in enumerate((row_0, row_1, row_2, row_3)):

        def visit_row(slot, carry, back=back, rows=rows):
            a = rows[2 * slot]
            w = rows[2 * slot + 1]
            one_at = buffer_of(REACH - back)
            two_at = buffer_of(REACH - back + w // OWN)
            last = jnp.maximum(one_at, two_at)
            phase = jnp.int32(0)
            for limit in LAST_BUFFER[:-1]:
                phase = phase + (last >= limit).astype(jnp.int32)
            for early in range(len(CAPS)):
                full = jnp.logical_and(phase == early, work[COUNTS, early] >= CAPS[early])
                phase = jnp.where(full, early + 1, phase)
            count = work[COUNTS, phase]
            work[2 * phase, count] = one_at * OWN + a
            work[2 * phase + 1, count] = two_at * OWN + w % OWN
            if back == 0:
                work[COUNTS, phase] = count + 1
            else:
                work[COUNTS, phase] = count + (w // OWN == back).astype(jnp.int32)
            return carry

        lax.fori_loop(0, rows[2 * SLOTS], visit_row, 0)


def planned(rows):
    smem = pl.BlockSpec(memory_space=pltpu.SMEM)
    return pl.pallas_call(
        plan,
        out_shape=jax.ShapeDtypeStruct((COUNTS + 1, (REACH + 1) * SLOTS + 1), jnp.int32),
        in_specs=[smem] * 4,
        out_specs=smem,
        name="plan",
    )(*rows)


def visit(phase, *refs):
    work = refs[0]
    held = LAST_BUFFER[phase]
    buffers = refs[1 : 1 + held]
    rest = list(refs[1 + held :])
    constants = [rest[0], rest[1].at[0], rest[1].at[1]]
    rest = rest[2:]
    before = rest.pop(0) if phase > 0 else None
    given = rest.pop(0)
    pair, rows, mixed, turned, stacked, result, sems, out_sems = rest[:8]
    total = rest[8] if phase == LAST else given
    found = work[COUNTS, phase]

    def fetch(item, slot):
        for side in range(2):
            code = work[2 * phase + side, item]
            at = code // OWN
            index = code % OWN
            for b in range(held):
                @pl.when(at == b)
                def _():
                    pltpu.make_async_copy(
                        buffers[b].at[index], pair.at[slot, side], sems.at[slot, side]
                    ).start()

    @pl.when(found > 0)
    def _():
        fetch(0, 0)

    if phase == 0:
        total[...] = jnp.zeros_like(total)
    if phase == LAST:
        total[...] = before[...]

    def step(item, carry):
        slot = item % 2
        for side in range(2):
            pltpu.make_async_copy(
                buffers[0].at[0], pair.at[slot, side], sems.at[slot, side]
            ).wait()

        @pl.when(item + 1 < found)
        def _():
            fetch(item + 1, 1 - slot)

        one = work[2 * phase, item]
        two = work[2 * phase + 1, item]
        both = pair.at[slot]
        own_one = one < OWN
        target = jnp.where(own_one, one, two)
        side = own_one.astype(jnp.int32)
        potential(
            both, (target, side), *constants, rows, mixed, turned, stacked, result, total
        )

        @pl.when(jnp.logical_and(jnp.logical_and(own_one, two < OWN), one != two))
        def _():
            take_away(total, two, result, both, 0)

        return carry

    lax.fori_loop(0, found, step, 0)
    if phase == LAST:
        copies = [
            pltpu.make_async_copy(total.at[k], given.at[k], out_sems.at[k]) for k in range(OWN)
        ]
        for copy in copies:
            copy.start()
        for copy in copies:
            copy.wait()


def visit_pairs(phase, work, buffers, constants, before):
    smem = pl.BlockSpec(memory_space=pltpu.SMEM)
    vmem = pl.BlockSpec(memory_space=pltpu.VMEM)
    anywhere = pl.BlockSpec(memory_space=pl.ANY)
    hbm = pl.BlockSpec(memory_space=pltpu.HBM)
    shape = (OWN, POINTS, POINTS * POINTS)
    extra = [] if before is None else [before]
    guess = 5
    return pl.pallas_call(
        functools.partial(visit, phase),
        out_shape=jax.ShapeDtypeStruct(shape, F32),
        in_specs=[smem, hbm] + [anywhere] * (len(buffers) - 1) + [vmem] * (2 + len(extra)),
        out_specs=hbm if phase == LAST else vmem,
        scratch_shapes=[
            pltpu.VMEM((2, 2, POINTS, POINTS * POINTS), BF16),
            pltpu.VMEM((POINTS * HALF, 256), BF16),
            pltpu.VMEM((HALF * PITCH_A, 128), F32),
            pltpu.VMEM((POINTS * PITCH_B, 128), F32),
            pltpu.VMEM((2 * POINTS, POINTS * POINTS), BF16),
            pltpu.VMEM((POINTS, POINTS * POINTS), F32),
            pltpu.SemaphoreType.DMA((2, 2)),
            pltpu.SemaphoreType.DMA((OWN,)),
        ]
        + ([pltpu.VMEM(shape, F32)] if phase == LAST else []),
        input_output_aliases={1 + len(buffers) + 2: 0} if 0 < phase < LAST else {},
        compiler_params=pltpu.CompilerParams(vmem_limit_bytes=24 << 20),
        cost_estimate=pl.CostEstimate(
            flops=guess * 3_000_000_000, bytes_accessed=guess << 20, transcendentals=0
        ),
    )(work, *buffers, *constants, *extra)


def moved(value, send):
    count = lax.axis_size("orb")
    return lax.ppermute(value, "orb", [(source, send(source) % count) for source in range(count)])


def swapped(value):
    return moved(value, lambda source: source ^ 1)


def outward(value):
    return moved(value, lambda source: source - 2 if source % 2 == 0 else source + 2)


def onward(value):
    return moved(value, lambda source: source - 1 if source % 2 == 0 else source + 1)


def exchange(orbitals, pair_list, pair_counts):
    sine, base = tables()
    row = jnp.concatenate([pair_list.reshape(-1), pair_counts])
    rows = [row]
    for k in range(1, REACH + 1):
        rows.append(moved(row, lambda source: source + k))
    first = outward(orbitals)
    beside = swapped(orbitals)
    work = planned(rows)
    constants = [sine, filled_tables(base)]

    def visited(phase, buffers, total):
        return visit_pairs(phase, work, buffers, constants, total)

    third = outward(beside)
    buffers = [orbitals, beside]
    total = visited(0, buffers, None)
    first, total = lax.optimization_barrier((first, total))
    second = onward(first)
    first_beside = swapped(first)
    buffers = buffers + [first]
    total = visited(1, buffers, total)
    buffers = buffers + [first_beside]
    total = visited(2, buffers, total)
    third, total = lax.optimization_barrier((third, total))
    third_beside = swapped(third)
    buffers = buffers + [third]
    total = visited(3, buffers, total)
    buffers = buffers + [third_beside]
    total = visited(4, buffers, total)
    return visited(5, buffers + [second], total)


def solution(mesh):
    return jax.shard_map(
        exchange,
        mesh=mesh,
        in_specs=(P("orb", None, None), P("orb", None), P("orb")),
        out_specs=P("orb", None, None),
        check_vma=False,
    )
```

```python
import functools
import math

import jax
import jax.numpy as jnp
import numpy as np
from jax import lax
from jax.experimental import pallas as pl
from jax.experimental.pallas import tpu as pltpu
from jax.sharding import PartitionSpec as P


REACH = 3
OWN = 4
SLOTS = 16
POINTS = 64
HALF = POINTS // 2
SCREENING = 0.5
LAST_BUFFER = (2, 3, 4, 5, 6, 7)
LAST = len(LAST_BUFFER) - 1
CAPS = (6, 5, 4)
COUNTS = 2 * LAST + 2
BF16 = jnp.bfloat16
F32 = jnp.float32


def split_table(table):
    high = table.astype(np.float32).astype(BF16)
    low = (table - high.astype(np.float64)).astype(np.float32).astype(BF16)
    return high, low


def tables():
    modes = np.arange(POINTS, dtype=np.float64) + 1.0
    sines = np.sin(math.pi * modes[:, None] * modes[None, :] / (POINTS + 1))
    high, low = split_table(sines)
    left_x = np.concatenate([high, high, low], 1)
    none = np.zeros((POINTS, POINTS), BF16)

    def twice(block):
        return np.block([[block, none], [none, block]])

    right_z = np.concatenate([np.concatenate([twice(high), twice(low)], 1)] * 2, 0)
    even, odd = sines[:HALF, 0::2], sines[:HALF, 1::2]

    def thrice(block):
        upper, lower = split_table(block)
        return np.concatenate([upper, upper, lower], 1)

    left_y = np.concatenate([thrice(even), thrice(odd)], 0)
    back_y = np.concatenate([thrice(even.T), thrice(odd.T)], 0)

    def wide(block):
        return np.pad(block, ((0, 0), (0, 256 - block.shape[1])))

    sine = np.concatenate([wide(left_x), wide(left_y), wide(back_y), right_z], 0)
    base = eigenvalues()[None, :] + eigenvalues()[:, None] + SCREENING
    base = np.concatenate([base, base], 1).astype(np.float32)
    return sine, np.stack([base[:HALF], base[::-1][:HALF]])


def eigenvalues():
    modes = np.arange(POINTS, dtype=np.float64) + 1.0
    return 4.0 * np.sin(math.pi * modes / (2.0 * (POINTS + 1))) ** 2


def parts(values):
    high = values.astype(BF16)
    low = (values - high.astype(F32)).astype(BF16)
    return high, low


def dot(left, right):
    return jnp.dot(left, right, preferred_element_type=F32)


def along_first(table, values):
    high, low = parts(values)
    return dot(table, jnp.concatenate([high, low, high], 0))


def along_last(rows, table):
    both = dot(rows, table)
    return both[:, :128] + both[:, 128:]


def side_by_side(values):
    high, low = parts(values)
    return jnp.concatenate([high, low], 1)


PITCH_A = 65
PITCH_B = 33


def forward_x(pair, sine, rows):
    left_x = sine[:POINTS, : 3 * POINTS]
    for c in range(16):
        lanes = pl.ds(c * 256, 256)
        density = pair[0, :, lanes].astype(F32) * pair[1, :, lanes].astype(F32)
        high, low = parts(along_first(left_x, density))
        for s in range(2):
            place = pl.ds((2 * c + s) * POINTS, POINTS)
            rows[place, :128] = high[:, 128 * s : 128 * s + 128]
            rows[place, 128:] = low[:, 128 * s : 128 * s + 128]


def forward_z(sine, rows, mixed):
    right_z = sine[3 * POINTS :, :]
    for c in range(8):
        out = along_last(rows[pl.ds(c * 256, 256), :], right_z)
        for s in range(4):
            mixed[pl.ds((4 * c + s) * PITCH_A, POINTS), :] = out[POINTS * s : POINTS * s + POINTS]


def both_y(sine, plus, minus, mixed, turned):
    left_y = sine[POINTS : 2 * POINTS, : 3 * HALF]
    back_y = sine[2 * POINTS : 3 * POINTS, : 3 * HALF]
    lane = lax.broadcasted_iota(jnp.int32, (HALF, 256), 1)
    first = (lane % 128) < 64
    for c in range(32):
        x = c * 2
        taken = [mixed[pl.ds(x + s, HALF, stride=PITCH_A), :] for s in range(2)]
        out = along_first(left_y, jnp.concatenate(taken, 1))
        held = jnp.where(first, out[:HALF], out[HALF:])
        other = jnp.concatenate(
            [pltpu.roll(held[:, :128], 64, 1), pltpu.roll(held[:, 128:], 64, 1)], 1
        )
        up = jnp.concatenate([plus[x], plus[x + 1]], 1)
        down = jnp.concatenate([minus[x], minus[x + 1]], 1)
        back = along_first(back_y, up * held + down * other)
        kept = jnp.where(first, back[:HALF], back[HALF:])
        for s in range(2):
            turned[pl.ds((x + s) * PITCH_B, HALF), :] = kept[:, 128 * s : 128 * s + 128]


def inverse_z(sine, turned, stacked):
    right_z = sine[3 * POINTS :, :]
    for c in range(8):
        taken = [side_by_side(turned[pl.ds(4 * c + s, POINTS, stride=PITCH_B), :]) for s in range(4)]
        high, low = parts(along_last(jnp.concatenate(taken, 0), right_z))
        for s in range(4):
            lanes = pl.ds((4 * c + s) * 128, 128)
            stacked[:POINTS, lanes] = high[POINTS * s : POINTS * s + POINTS]
            stacked[POINTS:, lanes] = low[POINTS * s : POINTS * s + POINTS]


def inverse_x(pair, target, sine, stacked, result, total):
    left_x = sine[:POINTS, : 3 * POINTS]
    position, side = target
    for c in range(16):
        lanes = pl.ds(c * 256, 256)
        high, low = stacked[:POINTS, lanes], stacked[POINTS:, lanes]
        out = dot(left_x, jnp.concatenate([high, low, high], 0))
        result[:, lanes] = out
        total[position, :, lanes] -= out * pair[side, :, lanes].astype(F32)


def take_away(total, position, result, pair, side):
    def step(c, carry):
        lanes = pl.ds(pl.multiple_of(c * 256, 256), 256)
        total[position, :, lanes] -= result[:, lanes] * pair[side, :, lanes].astype(F32)
        return carry

    lax.fori_loop(0, 16, step, 0, unroll=4)


def fill_tables(base, out):
    for x, value in enumerate(eigenvalues()):
        scale = (2.0 / (POINTS + 1)) ** 3
        near = scale / (base[0] + np.float32(value))
        far = scale / (base[1] + np.float32(value))
        out[0, x] = near + far
        out[1, x] = near - far


def filled_tables(base):
    vmem = pl.BlockSpec(memory_space=pltpu.VMEM)
    return pl.pallas_call(
        fill_tables,
        out_shape=jax.ShapeDtypeStruct((2, POINTS, HALF, 128), F32),
        in_specs=[vmem],
        out_specs=vmem,
        name="fill_tables",
    )(base)


def plan(row_0, row_1, row_2, row_3, work):
    odd = lax.axis_index("orb") % 2

    def buffer_of(place):
        evens = (6, 5, 3, 0, 1, 2, 4)
        odds = (4, 2, 1, 0, 3, 5, 6)
        at = jnp.int32(0)
        for k in range(2 * REACH + 1):
            at = jnp.where(place == k, jnp.where(odd == 1, odds[k], evens[k]), at)
        return at

    for phase in range(LAST + 1):
        work[COUNTS, phase] = 0
    for back, rows in enumerate((row_0, row_1, row_2, row_3)):

        def visit_row(slot, carry, back=back, rows=rows):
            a = rows[2 * slot]
            w = rows[2 * slot + 1]
            one_at = buffer_of(REACH - back)
            two_at = buffer_of(REACH - back + w // OWN)
            last = jnp.maximum(one_at, two_at)
            phase = jnp.int32(0)
            for limit in LAST_BUFFER[:-1]:
                phase = phase + (last >= limit).astype(jnp.int32)
            for early in range(len(CAPS)):
                full = jnp.logical_and(phase == early, work[COUNTS, early] >= CAPS[early])
                phase = jnp.where(full, early + 1, phase)
            count = work[COUNTS, phase]
            work[2 * phase, count] = one_at * OWN + a
            work[2 * phase + 1, count] = two_at * OWN + w % OWN
            if back == 0:
                work[COUNTS, phase] = count + 1
            else:
                work[COUNTS, phase] = count + (w // OWN == back).astype(jnp.int32)
            return carry

        lax.fori_loop(0, rows[2 * SLOTS], visit_row, 0)


def planned(rows):
    smem = pl.BlockSpec(memory_space=pltpu.SMEM)
    return pl.pallas_call(
        plan,
        out_shape=jax.ShapeDtypeStruct((COUNTS + 1, (REACH + 1) * SLOTS + 1), jnp.int32),
        in_specs=[smem] * 4,
        out_specs=smem,
        name="plan",
    )(*rows)


def visit(phase, *refs):
    work = refs[0]
    held = LAST_BUFFER[phase]
    buffers = refs[1 : 1 + held]
    rest = list(refs[1 + held :])
    constants = [rest[0], rest[1].at[0], rest[1].at[1]]
    sine, plus, minus = constants
    rest = rest[2:]
    before = rest.pop(0) if phase > 0 else None
    given = rest.pop(0)
    pair, rows, mixed, turned, stacked, result, sems, out_sems = rest[:8]
    total = rest[8] if phase == LAST else given
    found = work[COUNTS, phase]

    def fetch(item, slot):
        for side in range(2):
            code = work[2 * phase + side, item]
            at = code // OWN
            index = code % OWN
            for b in range(held):
                @pl.when(at == b)
                def _():
                    pltpu.make_async_copy(
                        buffers[b].at[index], pair.at[slot, side], sems.at[slot, side]
                    ).start()

    def arrive(slot):
        for side in range(2):
            pltpu.make_async_copy(
                buffers[0].at[0], pair.at[slot, side], sems.at[slot, side]
            ).wait()

    for early in range(2):
        @pl.when(found > early)
        def _():
            fetch(early, early)

    if phase == 0:
        total[...] = jnp.zeros_like(total)
    if phase == LAST:
        total[...] = before[...]

    def finish(item, slot, again):
        one = work[2 * phase, item]
        two = work[2 * phase + 1, item]
        own_one = one < OWN
        target = jnp.where(own_one, one, two)
        twice = jnp.logical_and(jnp.logical_and(own_one, two < OWN), one != two)
        return pair.at[slot], (target, own_one.astype(jnp.int32)), jnp.logical_and(twice, again), two

    def second_target(both, twice, two):
        @pl.when(twice)
        def _():
            take_away(total, two, result, both, 0)

    @pl.when(found > 0)
    def _():
        stacked[...] = jnp.zeros_like(stacked)

    def step(item, carry):
        slot = lax.rem(item, 3)
        last = jnp.maximum(item - 1, 0)
        arrive(slot)
        both, target, twice, two = finish(last, lax.rem(last, 3), item > 0)
        forward_x(pair.at[slot], sine, rows)
        forward_z(sine, rows, mixed)
        inverse_x(both, target, sine, stacked, result, total)
        both_y(sine, plus, minus, mixed, turned)
        inverse_z(sine, turned, stacked)
        second_target(both, twice, two)

        @pl.when(item + 2 < found)
        def _():
            fetch(item + 2, lax.rem(item + 2, 3))

        return carry

    lax.fori_loop(0, found, step, 0)

    @pl.when(found > 0)
    def _():
        both, target, twice, two = finish(found - 1, lax.rem(found - 1, 3), True)
        inverse_x(both, target, sine, stacked, result, total)
        second_target(both, twice, two)

    if phase == LAST:
        copies = [
            pltpu.make_async_copy(total.at[k], given.at[k], out_sems.at[k]) for k in range(OWN)
        ]
        for copy in copies:
            copy.start()
        for copy in copies:
            copy.wait()


def visit_pairs(phase, work, buffers, constants, before):
    smem = pl.BlockSpec(memory_space=pltpu.SMEM)
    vmem = pl.BlockSpec(memory_space=pltpu.VMEM)
    anywhere = pl.BlockSpec(memory_space=pl.ANY)
    hbm = pl.BlockSpec(memory_space=pltpu.HBM)
    shape = (OWN, POINTS, POINTS * POINTS)
    extra = [] if before is None else [before]
    guess = 5
    return pl.pallas_call(
        functools.partial(visit, phase),
        out_shape=jax.ShapeDtypeStruct(shape, F32),
        in_specs=[smem, hbm] + [anywhere] * (len(buffers) - 1) + [vmem] * (2 + len(extra)),
        out_specs=hbm if phase == LAST else vmem,
        scratch_shapes=[
            pltpu.VMEM((3, 2, POINTS, POINTS * POINTS), BF16),
            pltpu.VMEM((POINTS * HALF, 256), BF16),
            pltpu.VMEM((HALF * PITCH_A, 128), F32),
            pltpu.VMEM((POINTS * PITCH_B, 128), F32),
            pltpu.VMEM((2 * POINTS, POINTS * POINTS), BF16),
            pltpu.VMEM((POINTS, POINTS * POINTS), F32),
            pltpu.SemaphoreType.DMA((3, 2)),
            pltpu.SemaphoreType.DMA((OWN,)),
        ]
        + ([pltpu.VMEM(shape, F32)] if phase == LAST else []),
        input_output_aliases={1 + len(buffers) + 2: 0} if 0 < phase < LAST else {},
        compiler_params=pltpu.CompilerParams(vmem_limit_bytes=24 << 20),
        cost_estimate=pl.CostEstimate(
            flops=guess * 3_000_000_000, bytes_accessed=guess << 20, transcendentals=0
        ),
    )(work, *buffers, *constants, *extra)


def moved(value, send):
    count = lax.axis_size("orb")
    return lax.ppermute(value, "orb", [(source, send(source) % count) for source in range(count)])


def swapped(value):
    return moved(value, lambda source: source ^ 1)


def outward(value):
    return moved(value, lambda source: source - 2 if source % 2 == 0 else source + 2)


def onward(value):
    return moved(value, lambda source: source - 1 if source % 2 == 0 else source + 1)


def exchange(orbitals, pair_list, pair_counts):
    sine, base = tables()
    row = jnp.concatenate([pair_list.reshape(-1), pair_counts])
    rows = [row]
    for k in range(1, REACH + 1):
        rows.append(moved(row, lambda source: source + k))
    first = outward(orbitals)
    beside = swapped(orbitals)
    work = planned(rows)
    constants = [sine, filled_tables(base)]

    def visited(phase, buffers, total):
        return visit_pairs(phase, work, buffers, constants, total)

    third = outward(beside)
    buffers = [orbitals, beside]
    total = visited(0, buffers, None)
    first, total = lax.optimization_barrier((first, total))
    second = onward(first)
    first_beside = swapped(first)
    buffers = buffers + [first]
    total = visited(1, buffers, total)
    buffers = buffers + [first_beside]
    total = visited(2, buffers, total)
    third, total = lax.optimization_barrier((third, total))
    third_beside = swapped(third)
    buffers = buffers + [third]
    total = visited(3, buffers, total)
    buffers = buffers + [third_beside]
    total = visited(4, buffers, total)
    return visited(5, buffers + [second], total)


def solution(mesh):
    return jax.shard_map(
        exchange,
        mesh=mesh,
        in_specs=(P("orb", None, None), P("orb", None), P("orb")),
        out_specs=P("orb", None, None),
        check_vma=False,
    )
```
